32 devices in a mesh: lat: 8 (over z, y), lon: 4 (over x, core).
Axes of the slice: x: 2, y: 2, z: 4, core: 2. Of those that a mesh axis runs over, the one named last changes fastest.
Arguments:
- fields: bfloat16 [69, 128, 512], P(None, 'lat', 'lon'), may hold values from -6 to 6
- enc_kernel: bfloat16 [3, 3, 256, 69], replicated, may hold values from -0.25 to 0.25
- gen_kernel: bfloat16 [3, 3, 69, 256], replicated, may hold values from -0.125 to 0.125
- recon_grad: bfloat16 [69, 128, 512], P(None, 'lat', 'lon'), may hold values from -6 to 6
Outputs:
- rebuilt: bfloat16 [69, 128, 512], P(None, 'lat', 'lon')
- feat_grad: bfloat16 [256, 128, 512], P(None, 'lat', 'lon')
- enc_grad: float32 [3, 3, 256, 69], replicated
- gen_grad: float32 [3, 3, 69, 256], replicated
The draws below stay inside these ranges and needn't reach their ends.
All inputs are finite; a program needn't handle non-finite values.
Results may differ from the reference program's by a relative error of at most 0.0085.
Values may be sent and summed in bfloat16 or wider, within the bound.
A program may use at most 64 MiB of HBM per device.

```python
import jax
import jax.numpy as jnp
from jax import lax

CIN = 69
CH = 256
LAT = 128
LON = 512


def block_scale(key, extent, pieces, least, top_value):
    gain, own = 1.0, jax.random.fold_in(key, 6)
    for dim, parts in pieces:
        heights = jnp.exp(jax.random.uniform(jax.random.fold_in(own, dim), (parts,), jnp.float32, least / len(pieces), top_value / len(pieces)))
        gain = gain * jnp.repeat(heights, extent[dim] // parts).reshape([-1 if axis == dim else 1 for axis in range(len(extent))])
    return gain


def normal_values(key, extent, scale, most, cuts=(), dtype=jnp.bfloat16):
    gain = block_scale(key, extent, cuts, -0.22, 0.18) if cuts else 1.0
    drawn = jax.random.normal(key, extent, jnp.float32) * scale * gain
    return jnp.minimum(jnp.maximum(drawn, -most), most).astype(dtype)


def setup_inputs(seed: int = 0) -> dict:
    key_list = jax.random.split(jax.random.key(seed), 5)
    return {
        "fields": normal_values(key_list[0], (CIN, LAT, LON), 1.0, 6.0, ((1, 8), (2, 4))),
        "enc_kernel": normal_values(key_list[1], (3, 3, CH, CIN), (9 * CIN) ** -0.5, 0.25),
        "gen_kernel": normal_values(key_list[2], (3, 3, CIN, CH), (9 * CH) ** -0.5, 0.125),
        "recon_grad": normal_values(key_list[3], (CIN, LAT, LON), 1.0, 6.0, ((1, 8), (2, 4))),
    }


def pole_pad(source):
    lon_cells = source.shape[2]
    upper = jnp.roll(source[:, :1], lon_cells // 2, axis=2)
    lower = jnp.roll(source[:, -1:], lon_cells // 2, axis=2)
    stacked = jnp.concatenate([upper, source, lower], axis=1)
    return jnp.concatenate([stacked[:, :, -1:], stacked, stacked[:, :, :1]], axis=2)

def convolve(padded, kernel, height, width):
    running = jnp.zeros((kernel.shape[2], height * width), jnp.float32)
    for row_tap in range(3):
        for col_tap in range(3):
            section = padded[:, row_tap:row_tap + height, col_tap:col_tap + width].reshape(padded.shape[0], height * width)
            running = running + jnp.dot(kernel[row_tap, col_tap], section, preferred_element_type=jnp.float32)
    return running.reshape(kernel.shape[2], height, width)

def weight_grad(cotangent, padded, height, width):
    flat_cot = cotangent.reshape(cotangent.shape[0], height * width)
    taps = []
    for row_tap in range(3):
        row_list = []
        for col_tap in range(3):
            section = padded[:, row_tap:row_tap + height, col_tap:col_tap + width].reshape(padded.shape[0], height * width)
            row_list.append(lax.dot_general(flat_cot, section, (((1,), (1,)), ((), ())), preferred_element_type=jnp.float32))
        taps.append(jnp.stack(row_list))
    return jnp.stack(taps)

def adjoint_conv(cotangent, kernel, height, width):
    flat_cot = cotangent.reshape(cotangent.shape[0], height * width)
    spread = jnp.zeros((kernel.shape[3], height + 2, width + 2), jnp.float32)
    for row_tap in range(3):
        for col_tap in range(3):
            product = lax.dot_general(kernel[row_tap, col_tap], flat_cot, (((0,), (0,)), ((), ())), preferred_element_type=jnp.float32)
            spread = spread.at[:, row_tap:row_tap + height, col_tap:col_tap + width].add(product.reshape(kernel.shape[3], height, width))
    folded = spread[:, :, 1:-1]
    folded = folded.at[:, :, -1].add(spread[:, :, 0])
    folded = folded.at[:, :, 0].add(spread[:, :, -1])
    inner = folded[:, 1:-1]
    inner = inner.at[:, 0].add(jnp.roll(folded[:, 0], width // 2, axis=1))
    inner = inner.at[:, -1].add(jnp.roll(folded[:, -1], width // 2, axis=1))
    return inner

def reference(fields, enc_kernel, gen_kernel, recon_grad):
    height = fields.shape[1]
    width = fields.shape[2]
    padded_in = pole_pad(fields)
    pre_act = convolve(padded_in, enc_kernel, height, width)
    hidden = jax.nn.silu(pre_act).astype(jnp.bfloat16)
    padded_hid = pole_pad(hidden)
    rebuilt = convolve(padded_hid, gen_kernel, height, width).astype(jnp.bfloat16)
    feat_grad = adjoint_conv(recon_grad, gen_kernel, height, width).astype(jnp.bfloat16)
    logistic = jax.nn.sigmoid(pre_act)
    pre_grad = (feat_grad.astype(jnp.float32) * logistic * (1.0 + pre_act * (1.0 - logistic))).astype(jnp.bfloat16)
    norm_scale = 1.0 / jnp.sqrt(jnp.float32(LAT * LON))
    gen_grad = weight_grad(recon_grad, padded_hid, height, width) * norm_scale
    enc_grad = weight_grad(pre_grad, padded_in, height, width) * norm_scale
    return (rebuilt, feat_grad, enc_grad, gen_grad)
```

```python
import functools

import jax
import jax.numpy as jnp
from jax import lax
from jax.experimental import pallas as pl
from jax.experimental.pallas import tpu as pltpu
from jax.sharding import PartitionSpec as P

MESH = pl.DeviceIdType.MESH
LINK = jnp.bfloat16
F32 = jnp.float32
BF16 = jnp.bfloat16


def dot(left, right, dims):
    return lax.dot_general(left, right, (dims, ((), ())), preferred_element_type=F32)


def shifted(value, amount):
    width = value.shape[1]
    if isinstance(amount, int):
        amount = amount % width
        if amount == 0:
            return value
    return pltpu.roll(value, amount, 1)


def layer_kernel(
    lats, halves, deep, f_hbm, g_hbm, we_hbm, wg_hbm, reb_ref, feat_ref, grad_ref,
    fin, win, flat, xg, colp, colh, corner, hrow, dact, feat_rows, wpad, we, wf, wr,
    ysum, ycol, yhalo, turned, accx, accg, parts, from_pair, lon_out, from_lon, lat_out, from_lat,
    local_sem, *sems,
):
    count, height, width = fin.shape[1:]
    hid = hrow.shape[1]
    lons = 2 * halves
    band = 3 * deep
    half_deep = deep // 2
    lat = lax.axis_index("lat")
    lon = lax.axis_index("lon")
    half = lax.div(lon, 2)
    core = lax.rem(lon, 2)
    other = 1 - core
    below_top = lax.div(lat + lats - 1, lats)
    above_end = lax.div(2 * lats - 2 - lat, lats)

    def lon_peer(step):
        return (lat, lax.rem(half + step, halves) * 2 + core)

    def lat_peer(step):
        return (lax.rem(lat + step, lats), lon)

    def north_of(place):
        return (lat - below_top, lax.rem(place + (1 - below_top) * halves, lons))

    def south_of(place):
        return (lat + above_end, lax.rem(place + (1 - above_end) * halves, lons))

    west_lon = lax.rem(lon + lons - 1, lons)
    east_lon = lax.rem(lon + 1, lons)
    pair = (lat, half * 2 + other)
    west = (lat, west_lon)
    east = (lat, east_lon)
    north = north_of(lon)
    south = south_of(lon)
    diagonals = [
        (south_of(east_lon), 1 - above_end, 0),
        (north_of(east_lon), below_top, 0),
        (south_of(west_lon), 1 - above_end, 1),
        (north_of(west_lon), below_top, 1),
    ]

    barrier = pltpu.get_barrier_semaphore()
    peers = [west, east] + [peer for peer, slot, side in diagonals]
    peers += [lon_peer(step) for step in range(1, halves)]
    peers += [lat_peer(step) for step in range(1, lats)]
    for peer in peers:
        pl.semaphore_signal(barrier, inc=1, device_id=peer, device_id_type=MESH)

    loads = [
        pltpu.make_async_copy(f_hbm, fin.at[0], local_sem.at[0]),
        pltpu.make_async_copy(g_hbm, fin.at[1], local_sem.at[1]),
        pltpu.make_async_copy(we_hbm, win.at[0], local_sem.at[2]),
        pltpu.make_async_copy(wg_hbm, win.at[1], local_sem.at[3]),
    ]
    for load in loads:
        load.start()

    def send(src, dst, phase, send_slot, recv_slot, peer):
        copy = pltpu.make_async_remote_copy(
            src_ref=src,
            dst_ref=dst,
            send_sem=sems[2 * phase].at[send_slot],
            recv_sem=sems[2 * phase + 1].at[recv_slot],
            device_id=peer,
            device_id_type=MESH,
        )
        copy.start()
        return copy

    def arrive(ref, phase, slot):
        pltpu.make_async_copy(ref, ref, sems[2 * phase + 1].at[slot]).wait()

    lane = lax.broadcasted_iota(jnp.int32, (deep, width), 1)
    half_lane = lax.broadcasted_iota(jnp.int32, (half_deep, width), 1)
    rim = (lane == 0) | (lane == width - 1)

    for array in range(2):
        flat[array, count * height :] = jnp.zeros(((deep - count) * height, width), F32)
        wpad[array, :, deep - 16 :] = jnp.zeros((9, 16, hid), BF16)
    accx[...] = jnp.zeros_like(accx)
    accg[...] = jnp.zeros_like(accg)
    for load in loads[:2]:
        load.wait()
    for array in range(2):
        flat[array, : count * height] = fin[array].astype(F32).reshape(count * height, width)

    def cells_of(array, row):
        return flat[array, pl.ds(row, deep, stride=height), :]

    packed = jnp.zeros((half_deep, width), F32)
    for row in range(height):
        for array in range(2):
            cells = cells_of(array, row)
            xg[row + 1, array * band + deep : array * band + 2 * deep] = cells.astype(BF16)
            rims = jnp.where(rim, cells, 0.0)
            for part in range(2):
                packed = packed + shifted(
                    rims[part * half_deep : (part + 1) * half_deep],
                    2 * row + 1 + (2 * array + part) * 2 * height,
                )
    colp[...] = packed.astype(BF16)

    pl.semaphore_wait(barrier, len(peers))
    col_copies = [
        send(colp, colh.at[0], 12, 0, 0, east),
        send(colp, colh.at[1], 12, 1, 1, west),
    ]

    def send_rows(array):
        middle = pl.ds(array * band + deep, deep)
        return [
            send(
                xg.at[1, middle], xg.at[below_top * (height + 1), middle],
                13, 2 * array, 2 * array + below_top, north,
            ),
            send(
                xg.at[height, middle], xg.at[(1 - above_end) * (height + 1), middle],
                13, 2 * array + 1, 2 * array + 1 - above_end, south,
            ),
        ]

    row_copies = send_rows(0)
    corner_copies = [
        send(colp, corner.at[slot, side], 14, index, 2 * slot + side, peer)
        for index, (peer, slot, side) in enumerate(diagonals)
    ]
    row_copies += send_rows(1)

    for load in loads[2:]:
        load.wait()
    for array in range(2):
        for tap in range(9):
            row_tap, col_tap = divmod(tap, 3)
            target = (2 - row_tap) * 3 + col_tap if array else tap
            wpad[array, target, :count] = win[array, tap]
    for tap in range(9):
        row_tap, col_tap = divmod(tap, 3)
        wr[col_tap * deep : (col_tap + 1) * deep, row_tap * hid : (row_tap + 1) * hid] = wpad[
            1, (2 - row_tap) * 3 + col_tap
        ]
    line = lax.broadcasted_iota(jnp.int32, (hid, hid), 0)
    column = lax.broadcasted_iota(jnp.int32, (hid, hid), 1)
    eye = jnp.where(line == column, 1.0, 0.0).astype(BF16)
    for array, target in ((0, we), (1, wf)):
        target[...] = dot(eye, wpad[array].reshape(9 * deep, hid), ((1,), (1,))).astype(BF16)

    even = lax.rem(half_lane, 2) == 0

    def join(from_west, from_east):
        return jnp.where(
            even, shifted(from_east.astype(F32), -1), shifted(from_west.astype(F32), 1)
        )

    def widen(array, slot, cells, rims, turn):
        parts_in = []
        for part in range(2):
            group = (2 * array + part) * 2 * height
            parts_in.append(shifted(rims, turn(group)))
        edges = jnp.concatenate(parts_in, axis=0)
        before = jnp.where(lane == 0, edges, shifted(cells, 1)).astype(BF16)
        after = jnp.where(lane == width - 1, edges, shifted(cells, -1)).astype(BF16)
        first, last = (after, before) if array else (before, after)
        base = array * band
        xg[slot, base : base + deep] = first
        xg[slot, base + 2 * deep : base + band] = last

    for copy in col_copies:
        copy.wait()
    own_rims = join(colh[0], colh[1])

    def widen_own(array):
        for row in range(height):
            widen(
                array, row + 1, cells_of(array, row), own_rims,
                lambda group: -(2 * row + 1 + group),
            )

    widen_own(0)
    for copy in corner_copies:
        copy.wait_send()
    for slot in range(4):
        arrive(corner.at[slot // 2, slot % 2], 14, slot)
    for copy in row_copies:
        copy.wait_send()
    halo_rims = [join(corner[slot, 0], corner[slot, 1]) for slot in range(2)]
    source_rows = (below_top * (height - 1), (1 - above_end) * (height - 1))

    def widen_halo(array):
        middle = pl.ds(array * band + deep, deep)
        for slot in range(2):
            arrive(xg.at[slot * (height + 1), middle], 13, 2 * array + slot)
        for slot in range(2):
            cells = xg[slot * (height + 1), array * band + deep : array * band + 2 * deep]
            at = source_rows[slot]
            widen(
                array, slot * (height + 1), cells.astype(F32), halo_rims[slot],
                lambda group: lax.rem(2 * width - (2 * at + 1 + group), width),
            )

    widen_halo(0)
    widen_own(1)
    widen_halo(1)

    ends = ((0, below_top, 2 * band, 0), (1, above_end, 0, height - 1))
    at_poles = []
    for slot, inside, start, row in ends:
        edge = xg[slot * (height + 1), band:]
        at_poles.append(jnp.where(inside == 0, edge, jnp.zeros_like(edge)))
        xg[slot * (height + 1), band:] = jnp.where(inside == 0, jnp.zeros_like(edge), edge)

    rows = 4
    steps = height // rows

    def window(ref, row, start, size):
        return jnp.concatenate(
            [
                ref[pl.ds(row + place, 3), start : start + size].reshape(3 * size, width)
                for place in range(rows)
            ],
            axis=1,
        )

    def first_step(step):
        row = step * rows
        pre_act = dot(we[...], window(xg, row, 0, band), ((1,), (0,)))
        logistic = 1.0 / (1.0 + jnp.exp(-pre_act))
        gated = pre_act * logistic
        dact[step] = logistic + gated * (1.0 - logistic)
        hidden = gated.astype(BF16)
        for place in range(rows):
            hrow[row + 1 + place] = hidden[:, place * width : (place + 1) * width]
        accg[...] += dot(window(xg, row, band, band), hidden, ((1,), (1,)))

    def second_step(step, extra):
        row = step * rows
        feat = dot(wf[...], window(xg, row, band, band), ((1,), (0,)))
        if extra is not None:
            feat = feat + extra
        feat = feat.astype(BF16)
        for place in range(rows):
            feat_rows[row + place] = feat[:, place * width : (place + 1) * width]
        pre_grad = (feat.astype(F32) * dact[step]).astype(BF16)
        accx[...] += dot(window(xg, row, 0, band), pre_grad, ((1,), (1,)))

    for step in range(steps):
        first_step(step)
    hid_copies = [
        send(hrow.at[1], hrow.at[below_top * (height + 1)], 15, 0, below_top, north),
        send(hrow.at[height], hrow.at[(1 - above_end) * (height + 1)], 15, 1, 1 - above_end, south),
    ]
    for slot, inside, start, row in ends:
        accg[start : start + band] += dot(at_poles[slot], hrow[row + 1], ((1,), (1,)))

    side_lanes = hid // 2
    per = lon_out.shape[2]

    def fill(stream, acc, backward):
        used = 9 * count
        for tap in range(9):
            row_tap, col_tap = divmod(tap, 3)
            source = ((2 - row_tap) * 3 + col_tap if backward else tap) * deep
            for side in range(2):
                parts[stream, side, tap * count : (tap + 1) * count] = acc[
                    source : source + count, side * side_lanes : (side + 1) * side_lanes
                ]
        spare = parts.shape[2] - used
        if spare:
            for side in range(2):
                parts[stream, side, used:] = jnp.zeros((spare, side_lanes), F32)

    def piece(index, size):
        return pl.ds(pl.multiple_of(index * size, 8), size)

    order = sorted(range(1, lats), key=lambda step: abs(2 * step - lats))

    def start_pair(stream):
        copies = {}
        for step in list(range(1, halves)) + [0]:
            part = piece(lax.rem(half + step, halves), lats * per)
            copies[step] = send(
                parts.at[stream, other, part], from_pair.at[stream, part], stream * 6, step, step, pair
            )
        return copies

    def start_lon(stream, copies):
        onward = {}
        for step in range(1, halves):
            copies[step].wait()
            target = lax.rem(half + step, halves)
            for turn in order + [0]:
                there = lax.rem(lat + turn, lats)
                chunk = target * lats + there
                part = piece(chunk, per)
                lon_out[stream, chunk] = (
                    parts[stream, core, part] + from_pair[stream, part]
                ).astype(LINK)
                onward[step, turn] = send(
                    lon_out.at[stream, chunk],
                    from_lon.at[stream, step - 1, there],
                    stream * 6 + 1, (step - 1) * lats + turn, (step - 1) * lats + turn, lon_peer(step),
                )
        copies[0].wait()
        return onward

    def lon_total(stream, copies, turn):
        there = lax.rem(lat + turn, lats)
        part = piece(half * lats + there, per)
        total = parts[stream, core, part] + from_pair[stream, part]
        for step in range(1, halves):
            copies[step, turn].wait()
            total = total + from_lon[stream, step - 1, there].astype(F32)
        return total

    def start_lat(stream, copies):
        onward = []
        for turn in order:
            there = lax.rem(lat + turn, lats)
            lat_out[stream, there] = lon_total(stream, copies, turn).astype(LINK)
            onward.append(
                send(
                    lat_out.at[stream, there], from_lat.at[stream, turn - 1],
                    stream * 6 + 2, turn - 1, turn - 1, lat_peer(turn),
                )
            )
        return onward, lon_total(stream, copies, 0)

    def spread(stream, turn, lon_copies, pair_copies):
        there = lax.rem(lat + lats - turn, lats)
        mine = grad_ref.at[stream, core, half * lats + there]
        for step in range(1, halves):
            slot = (step - 1) * lats + turn
            lon_copies[step, turn] = send(mine, mine, stream * 6 + 4, slot, slot, lon_peer(step))
        pair_copies.append(send(mine, mine, stream * 6 + 5, turn, turn, pair))

    def start_lat_gather(stream, started):
        copies, total = started
        for turn, copy in zip(order, copies):
            copy.wait()
            total = total + from_lat[stream, turn - 1].astype(F32)
        place = half * lats + lat
        grad_ref[stream, core, place] = total.astype(grad_ref.dtype)
        mine = grad_ref.at[stream, core, place]
        copies = [
            send(mine, mine, stream * 6 + 3, turn - 1, turn - 1, lat_peer(turn)) for turn in order
        ]
        lon_copies, pair_copies = {}, []
        spread(stream, 0, lon_copies, pair_copies)
        return copies, lon_copies, pair_copies

    def start_spread(stream, started):
        copies, lon_copies, pair_copies = started
        for turn, copy in reversed(list(zip(order, copies))):
            copy.wait()
            spread(stream, turn, lon_copies, pair_copies)
        return lon_copies, pair_copies

    def start_pair_gather(stream, started):
        lon_copies, pair_copies = started
        for turn in [0] + order[::-1]:
            for step in range(1, halves):
                lon_copies[step, turn].wait()
                source = lax.rem(half + halves - step, halves)
                there = lax.rem(lat + lats - turn, lats)
                mine = grad_ref.at[stream, core, source * lats + there]
                slot = step * lats + turn
                pair_copies.append(send(mine, mine, stream * 6 + 5, slot, slot, pair))
        return pair_copies

    def pole_term(slot, start):
        return dot(wf[:, start : start + band], at_poles[slot], ((1,), (0,)))

    fill(0, accg, True)
    gen_copies = start_pair(0)
    open_gap = jnp.zeros((hid, (rows - 1) * width), F32)
    for step in range(steps):
        extra = None
        if step == 0:
            extra = jnp.concatenate([pole_term(0, 2 * band), open_gap], axis=1)
        elif step == steps - 1:
            extra = jnp.concatenate([open_gap, pole_term(1, 0)], axis=1)
        second_step(step, extra)
        if step == 1:
            gen_copies = start_lon(0, gen_copies)
    fill(1, accx, False)
    enc_copies = start_pair(1)

    for copy in hid_copies:
        copy.wait_send()
    for slot in range(2):
        arrive(hrow.at[slot * (height + 1)], 15, slot)

    def rebuild_step(step, packed):
        value = dot(wr[...], window(hrow, step * rows, 0, hid), ((1,), (0,)))
        for place in range(rows):
            row = step * rows + place
            lanes = slice(place * width, (place + 1) * width)
            left, centre, right = (value[tap * deep : (tap + 1) * deep, lanes] for tap in range(3))
            packed = packed + shifted(
                jnp.where(lane == width - 1, left, jnp.where(lane == 0, right, 0.0)), 2 * row + 1
            )
            inner = jnp.where(lane == 0, 0.0, shifted(left, 1))
            inner = inner + centre
            inner = inner + jnp.where(lane == width - 1, 0.0, shifted(right, -1))
            ysum[row] = inner
        return packed

    packed = jnp.zeros((deep, width), F32)
    packed = rebuild_step(0, packed)
    enc_copies = start_lon(1, enc_copies)
    gen_copies = start_lat(0, gen_copies)
    for step in range(1, steps):
        packed = rebuild_step(step, packed)
    ycol[...] = packed
    y_copies = [
        send(ycol, yhalo.at[0], 16, 0, 0, east),
        send(ycol, yhalo.at[1], 16, 1, 1, west),
    ]
    enc_copies = start_lat(1, enc_copies)

    def turn_out(load, target, size):
        for row in range(height):
            turned[pl.ds(row, size, stride=height), :] = load(row)
        target[...] = turned[: target.shape[0] * height].reshape(target.shape).astype(BF16)

    turn_out(lambda row: feat_rows[row].astype(F32), feat_ref, hid)
    gen_copies = start_lat_gather(0, gen_copies)
    for copy in y_copies:
        copy.wait()
    y_rims = jnp.where(lax.rem(lane, 2) == 0, shifted(yhalo[1], -1), shifted(yhalo[0], 1))

    def rebuilt_row(row):
        edges = shifted(y_rims, -(2 * row + 1))
        return ysum[row] + jnp.where((lane == 0) | (lane == width - 1), edges, 0.0)

    turn_out(rebuilt_row, reb_ref, deep)
    enc_copies = start_lat_gather(1, enc_copies)
    gen_copies = start_spread(0, gen_copies)
    gen_copies = start_pair_gather(0, gen_copies)
    enc_copies = start_spread(1, enc_copies)
    enc_copies = start_pair_gather(1, enc_copies)
    for copy in gen_copies + enc_copies:
        copy.wait()


def finish_kernel(norm, reb_in, feat_in, grad_in, reb_out, feat_out, enc_out, gen_out, flat, ready, sem):
    taps, count, hid = enc_out.shape
    side_lanes = hid // 2
    copies = [
        pltpu.make_async_copy(feat_in, feat_out, sem.at[0]),
        pltpu.make_async_copy(reb_in, reb_out, sem.at[1]),
    ]
    for copy in copies:
        copy.start()
    for stream, out in ((0, gen_out), (1, enc_out)):
        for side in range(2):
            gathered = grad_in[stream, side].astype(F32) * norm
            flat[:, side * side_lanes : (side + 1) * side_lanes] = gathered.reshape(-1, side_lanes)
        for tap in range(taps):
            ready[stream, tap] = flat[tap * count : (tap + 1) * count]
        copies.append(pltpu.make_async_copy(ready.at[stream], out, sem.at[2 + stream]))
        copies[-1].start()
    for copy in copies:
        copy.wait()


def on_device(fields, enc_kernel, gen_kernel, recon_grad):
    count, height, width = fields.shape
    hid = enc_kernel.shape[2]
    deep = -(-count // 16) * 16
    lats = lax.axis_size("lat")
    lons = lax.axis_size("lon")
    halves = lons // 2
    band = 3 * deep
    side_lanes = hid // 2
    chunks = halves * lats
    per = -(-9 * count // (chunks * 8)) * 8
    hops = (halves - 1) * lats
    counts = [halves, hops, lats - 1, lats - 1, hops, chunks] * 2 + [2, 4, 4, 2, 2]
    vmem = pl.BlockSpec(memory_space=pltpu.VMEM)
    anywhere = pl.BlockSpec(memory_space=pltpu.HBM)
    rebuilt, feat, summed = pl.pallas_call(
        functools.partial(layer_kernel, lats, halves, deep),
        out_shape=[
            jax.ShapeDtypeStruct((count, height, width), BF16),
            jax.ShapeDtypeStruct((hid, height, width), BF16),
            jax.ShapeDtypeStruct((2, 2, chunks, per, side_lanes), BF16),
        ],
        in_specs=[anywhere] * 4,
        out_specs=[vmem] * 3,
        scratch_shapes=[
            pltpu.VMEM((2, count, height, width), BF16),
            pltpu.VMEM((2, 9, count, hid), BF16),
            pltpu.VMEM((2, deep * height, width), F32),
            pltpu.VMEM((height + 2, 2 * band, width), BF16),
            pltpu.VMEM((deep // 2, width), BF16),
            pltpu.VMEM((2, deep // 2, width), BF16),
            pltpu.VMEM((2, 2, deep // 2, width), BF16),
            pltpu.VMEM((height + 2, hid, width), BF16),
            pltpu.VMEM((height // 4, hid, 4 * width), F32),
            pltpu.VMEM((height, hid, width), BF16),
            pltpu.VMEM((2, 9, deep, hid), BF16),
            pltpu.VMEM((hid, 9 * deep), BF16),
            pltpu.VMEM((hid, 9 * deep), BF16),
            pltpu.VMEM((band, 3 * hid), BF16),
            pltpu.VMEM((height, deep, width), F32),
            pltpu.VMEM((deep, width), F32),
            pltpu.VMEM((2, deep, width), F32),
            pltpu.VMEM((hid * height, width), F32),
            pltpu.VMEM((9 * deep, hid), F32),
            pltpu.VMEM((9 * deep, hid), F32),
            pltpu.VMEM((2, 2, chunks * per, side_lanes), F32),
            pltpu.VMEM((2, chunks * per, side_lanes), F32),
            pltpu.VMEM((2, chunks, per, side_lanes), LINK),
            pltpu.VMEM((2, halves - 1, lats, per, side_lanes), LINK),
            pltpu.VMEM((2, lats, per, side_lanes), LINK),
            pltpu.VMEM((2, lats - 1, per, side_lanes), LINK),
            pltpu.SemaphoreType.DMA((4,)),
        ]
        + [pltpu.SemaphoreType.DMA((size,)) for size in counts for _ in range(2)],
        compiler_params=pltpu.CompilerParams(
            collective_id=0, has_side_effects=True, vmem_limit_bytes=48 << 20
        ),
    )(
        fields,
        recon_grad,
        enc_kernel.transpose(0, 1, 3, 2).reshape(9, count, hid),
        gen_kernel.reshape(9, count, hid),
    )
    norm = 1.0 / float(height * lats * width * lons) ** 0.5
    rebuilt, feat, enc_grad, gen_grad = pl.pallas_call(
        functools.partial(finish_kernel, norm),
        out_shape=[
            jax.ShapeDtypeStruct((count, height, width), BF16),
            jax.ShapeDtypeStruct((hid, height, width), BF16),
            jax.ShapeDtypeStruct((9, count, hid), F32),
            jax.ShapeDtypeStruct((9, count, hid), F32),
        ],
        in_specs=[vmem] * 3,
        out_specs=[anywhere] * 4,
        scratch_shapes=[
            pltpu.VMEM((chunks * per, hid), F32),
            pltpu.VMEM((2, 9, count, hid), F32),
            pltpu.SemaphoreType.DMA((4,)),
        ],
    )(rebuilt, feat, summed)
    return (
        rebuilt,
        feat,
        enc_grad.reshape(3, 3, count, hid).transpose(0, 1, 3, 2),
        gen_grad.reshape(3, 3, count, hid),
    )


def solution(mesh):
    return jax.shard_map(
        on_device,
        mesh=mesh,
        in_specs=(P(None, "lat", "lon"), P(), P(), P(None, "lat", "lon")),
        out_specs=(P(None, "lat", "lon"), P(None, "lat", "lon"), P(), P()),
        check_vma=False,
    )
```

```python
import functools

import jax
import jax.numpy as jnp
from jax import lax
from jax.experimental import pallas as pl
from jax.experimental.pallas import tpu as pltpu
from jax.sharding import PartitionSpec as P

MESH = pl.DeviceIdType.MESH
LINK = jnp.bfloat16
F32 = jnp.float32
BF16 = jnp.bfloat16


def dot(left, right, dims):
    return lax.dot_general(left, right, (dims, ((), ())), preferred_element_type=F32)


def shifted(value, amount):
    width = value.shape[1]
    if isinstance(amount, int):
        amount = amount % width
        if amount == 0:
            return value
    return pltpu.roll(value, amount, 1)


def layer_kernel(
    lats, halves, deep, f_hbm, g_hbm, we_hbm, wg_hbm, reb_ref, feat_ref, grad_ref,
    fin, win, flat, xg, colp, colh, corner, hrow, dact, feat_rows, wpad, we, wf, wr,
    ysum, ycol, yhalo, turned, accx, accg, parts, from_pair, lon_out, from_lon, lat_out, from_lat,
    local_sem, *sems,
):
    count, height, width = fin.shape[1:]
    hid = hrow.shape[1]
    lons = 2 * halves
    band = 3 * deep
    half_deep = deep // 2
    lat = lax.axis_index("lat")
    lon = lax.axis_index("lon")
    half = lax.div(lon, 2)
    core = lax.rem(lon, 2)
    other = 1 - core
    below_top = lax.div(lat + lats - 1, lats)
    above_end = lax.div(2 * lats - 2 - lat, lats)

    def lon_peer(step):
        return (lat, lax.rem(half + step, halves) * 2 + core)

    def lat_peer(step):
        return (lax.rem(lat + step, lats), lon)

    def north_of(place):
        return (lat - below_top, lax.rem(place + (1 - below_top) * halves, lons))

    def south_of(place):
        return (lat + above_end, lax.rem(place + (1 - above_end) * halves, lons))

    west_lon = lax.rem(lon + lons - 1, lons)
    east_lon = lax.rem(lon + 1, lons)
    pair = (lat, half * 2 + other)
    west = (lat, west_lon)
    east = (lat, east_lon)
    north = north_of(lon)
    south = south_of(lon)
    diagonals = [
        (south_of(east_lon), 1 - above_end, 0),
        (north_of(east_lon), below_top, 0),
        (south_of(west_lon), 1 - above_end, 1),
        (north_of(west_lon), below_top, 1),
    ]

    barrier = pltpu.get_barrier_semaphore()
    peers = [west, east] + [peer for peer, slot, side in diagonals]
    peers += [lon_peer(step) for step in range(1, halves)]
    peers += [lat_peer(step) for step in range(1, lats)]
    for peer in peers:
        pl.semaphore_signal(barrier, inc=1, device_id=peer, device_id_type=MESH)

    loads = [
        pltpu.make_async_copy(f_hbm, fin.at[0], local_sem.at[0]),
        pltpu.make_async_copy(g_hbm, fin.at[1], local_sem.at[1]),
        pltpu.make_async_copy(we_hbm, win.at[0], local_sem.at[2]),
        pltpu.make_async_copy(wg_hbm, win.at[1], local_sem.at[3]),
    ]
    for load in loads:
        load.start()

    def send(src, dst, phase, send_slot, recv_slot, peer):
        copy = pltpu.make_async_remote_copy(
            src_ref=src,
            dst_ref=dst,
            send_sem=sems[2 * phase].at[send_slot],
            recv_sem=sems[2 * phase + 1].at[recv_slot],
            device_id=peer,
            device_id_type=MESH,
        )
        copy.start()
        return copy

    def arrive(ref, phase, slot):
        pltpu.make_async_copy(ref, ref, sems[2 * phase + 1].at[slot]).wait()

    lane = lax.broadcasted_iota(jnp.int32, (deep, width), 1)
    half_lane = lax.broadcasted_iota(jnp.int32, (half_deep, width), 1)
    rim = (lane == 0) | (lane == width - 1)

    for array in range(2):
        flat[array, count * height :] = jnp.zeros(((deep - count) * height, width), F32)
        wpad[array, :, deep - 16 :] = jnp.zeros((9, 16, hid), BF16)
    accx[...] = jnp.zeros_like(accx)
    accg[...] = jnp.zeros_like(accg)
    for load in loads[:2]:
        load.wait()
    for array in range(2):
        flat[array, : count * height] = fin[array].astype(F32).reshape(count * height, width)

    def cells_of(array, row):
        return flat[array, pl.ds(row, deep, stride=height), :]

    packed = jnp.zeros((half_deep, width), F32)
    for row in range(height):
        for array in range(2):
            cells = cells_of(array, row)
            xg[row + 1, array * band + deep : array * band + 2 * deep] = cells.astype(BF16)
            rims = jnp.where(rim, cells, 0.0)
            for part in range(2):
                packed = packed + shifted(
                    rims[part * half_deep : (part + 1) * half_deep],
                    2 * row + 1 + (2 * array + part) * 2 * height,
                )
    colp[...] = packed.astype(BF16)

    pl.semaphore_wait(barrier, len(peers))
    col_copies = [
        send(colp, colh.at[0], 12, 0, 0, east),
        send(colp, colh.at[1], 12, 1, 1, west),
    ]

    def send_rows(array):
        middle = pl.ds(array * band + deep, deep)
        return [
            send(
                xg.at[1, middle], xg.at[below_top * (height + 1), middle],
                13, 2 * array, 2 * array + below_top, north,
            ),
            send(
                xg.at[height, middle], xg.at[(1 - above_end) * (height + 1), middle],
                13, 2 * array + 1, 2 * array + 1 - above_end, south,
            ),
        ]

    row_copies = send_rows(0)
    corner_copies = [
        send(colp, corner.at[slot, side], 14, index, 2 * slot + side, peer)
        for index, (peer, slot, side) in enumerate(diagonals)
    ]
    row_copies += send_rows(1)

    for load in loads[2:]:
        load.wait()
    for array in range(2):
        for tap in range(9):
            row_tap, col_tap = divmod(tap, 3)
            target = (2 - row_tap) * 3 + col_tap if array else tap
            wpad[array, target, :count] = win[array, tap]
    for tap in range(9):
        row_tap, col_tap = divmod(tap, 3)
        wr[col_tap * deep : (col_tap + 1) * deep, row_tap * hid : (row_tap + 1) * hid] = wpad[
            1, (2 - row_tap) * 3 + col_tap
        ]
    line = lax.broadcasted_iota(jnp.int32, (hid, hid), 0)
    column = lax.broadcasted_iota(jnp.int32, (hid, hid), 1)
    eye = jnp.where(line == column, 1.0, 0.0).astype(BF16)
    for array, target in ((0, we), (1, wf)):
        target[...] = dot(eye, wpad[array].reshape(9 * deep, hid), ((1,), (1,))).astype(BF16)

    even = lax.rem(half_lane, 2) == 0

    def join(from_west, from_east):
        return jnp.where(
            even, shifted(from_east.astype(F32), -1), shifted(from_west.astype(F32), 1)
        )

    def widen(array, slot, cells, rims, turn):
        parts_in = []
        for part in range(2):
            group = (2 * array + part) * 2 * height
            parts_in.append(shifted(rims, turn(group)))
        edges = jnp.concatenate(parts_in, axis=0)
        before = jnp.where(lane == 0, edges, shifted(cells, 1)).astype(BF16)
        after = jnp.where(lane == width - 1, edges, shifted(cells, -1)).astype(BF16)
        first, last = (after, before) if array else (before, after)
        base = array * band
        xg[slot, base : base + deep] = first
        xg[slot, base + 2 * deep : base + band] = last

    for copy in col_copies:
        copy.wait()
    own_rims = join(colh[0], colh[1])

    def widen_own(array):
        for row in range(height):
            widen(
                array, row + 1, cells_of(array, row), own_rims,
                lambda group: -(2 * row + 1 + group),
            )

    widen_own(0)
    for copy in corner_copies:
        copy.wait_send()
    for slot in range(4):
        arrive(corner.at[slot // 2, slot % 2], 14, slot)
    for copy in row_copies:
        copy.wait_send()
    halo_rims = [join(corner[slot, 0], corner[slot, 1]) for slot in range(2)]
    source_rows = (below_top * (height - 1), (1 - above_end) * (height - 1))

    def widen_halo(array):
        middle = pl.ds(array * band + deep, deep)
        for slot in range(2):
            arrive(xg.at[slot * (height + 1), middle], 13, 2 * array + slot)
        for slot in range(2):
            cells = xg[slot * (height + 1), array * band + deep : array * band + 2 * deep]
            at = source_rows[slot]
            widen(
                array, slot * (height + 1), cells.astype(F32), halo_rims[slot],
                lambda group: lax.rem(2 * width - (2 * at + 1 + group), width),
            )

    widen_halo(0)
    widen_own(1)
    widen_halo(1)

    ends = ((0, below_top, 2 * band, 0), (1, above_end, 0, height - 1))
    at_poles = []
    for slot, inside, start, row in ends:
        edge = xg[slot * (height + 1), band:]
        at_poles.append(jnp.where(inside == 0, edge, jnp.zeros_like(edge)))
        xg[slot * (height + 1), band:] = jnp.where(inside == 0, jnp.zeros_like(edge), edge)

    rows = 4
    steps = height // rows

    def window(ref, row, start, size):
        return jnp.concatenate(
            [
                ref[pl.ds(row + place, 3), start : start + size].reshape(3 * size, width)
                for place in range(rows)
            ],
            axis=1,
        )

    def first_step(step):
        row = step * rows
        pre_act = dot(we[...], window(xg, row, 0, band), ((1,), (0,)))
        logistic = 1.0 / (1.0 + jnp.exp(-pre_act))
        gated = pre_act * logistic
        dact[step] = logistic + gated * (1.0 - logistic)
        hidden = gated.astype(BF16)
        for place in range(rows):
            hrow[row + 1 + place] = hidden[:, place * width : (place + 1) * width]
        accg[...] += dot(window(xg, row, band, band), hidden, ((1,), (1,)))

    def second_step(step, extra):
        row = step * rows
        feat = dot(wf[...], window(xg, row, band, band), ((1,), (0,)))
        if extra is not None:
            feat = feat + extra
        feat = feat.astype(BF16)
        for place in range(rows):
            feat_rows[row + place] = feat[:, place * width : (place + 1) * width]
        pre_grad = (feat.astype(F32) * dact[step]).astype(BF16)
        accx[...] += dot(window(xg, row, 0, band), pre_grad, ((1,), (1,)))

    for step in range(steps):
        first_step(step)
    hid_copies = [
        send(hrow.at[1], hrow.at[below_top * (height + 1)], 15, 0, below_top, north),
        send(hrow.at[height], hrow.at[(1 - above_end) * (height + 1)], 15, 1, 1 - above_end, south),
    ]
    for slot, inside, start, row in ends:
        accg[start : start + band] += dot(at_poles[slot], hrow[row + 1], ((1,), (1,)))

    side_lanes = hid // 2
    per = lon_out.shape[2]

    def fill(stream, acc, backward):
        used = 9 * count
        for tap in range(9):
            row_tap, col_tap = divmod(tap, 3)
            source = ((2 - row_tap) * 3 + col_tap if backward else tap) * deep
            for side in range(2):
                parts[stream, side, tap * count : (tap + 1) * count] = acc[
                    source : source + count, side * side_lanes : (side + 1) * side_lanes
                ]
        spare = parts.shape[2] - used
        if spare:
            for side in range(2):
                parts[stream, side, used:] = jnp.zeros((spare, side_lanes), F32)

    def piece(index, size):
        return pl.ds(pl.multiple_of(index * size, 8), size)

    order = sorted(range(1, lats), key=lambda step: abs(2 * step - lats))

    def start_pair(stream):
        copies = {}
        for step in list(range(1, halves)) + [0]:
            part = piece(lax.rem(half + step, halves), lats * per)
            copies[step] = send(
                parts.at[stream, other, part], from_pair.at[stream, part], stream * 6, step, step, pair
            )
        return copies

    def start_lon(stream, copies):
        onward = {}
        for step in range(1, halves):
            copies[step].wait()
            target = lax.rem(half + step, halves)
            for turn in order + [0]:
                there = lax.rem(lat + turn, lats)
                chunk = target * lats + there
                part = piece(chunk, per)
                lon_out[stream, chunk] = (
                    parts[stream, core, part] + from_pair[stream, part]
                ).astype(LINK)
                onward[step, turn] = send(
                    lon_out.at[stream, chunk],
                    from_lon.at[stream, step - 1, there],
                    stream * 6 + 1, (step - 1) * lats + turn, (step - 1) * lats + turn, lon_peer(step),
                )
        copies[0].wait()
        return onward

    def lon_total(stream, copies, turn):
        there = lax.rem(lat + turn, lats)
        part = piece(half * lats + there, per)
        total = parts[stream, core, part] + from_pair[stream, part]
        for step in range(1, halves):
            copies[step, turn].wait()
            total = total + from_lon[stream, step - 1, there].astype(F32)
        return total

    def start_lat(stream, copies):
        onward = []
        for turn in order:
            there = lax.rem(lat + turn, lats)
            lat_out[stream, there] = lon_total(stream, copies, turn).astype(LINK)
            onward.append(
                send(
                    lat_out.at[stream, there], from_lat.at[stream, turn - 1],
                    stream * 6 + 2, turn - 1, turn - 1, lat_peer(turn),
                )
            )
        return onward, lon_total(stream, copies, 0)

    def spread(stream, turn, lon_copies, pair_copies):
        there = lax.rem(lat + lats - turn, lats)
        mine = grad_ref.at[stream, core, half * lats + there]
        for step in range(1, halves):
            slot = (step - 1) * lats + turn
            lon_copies[step, turn] = send(mine, mine, stream * 6 + 4, slot, slot, lon_peer(step))
        pair_copies.append(send(mine, mine, stream * 6 + 5, turn, turn, pair))

    def start_lat_gather(stream, started):
        copies, total = started
        for turn, copy in zip(order, copies):
            copy.wait()
            total = total + from_lat[stream, turn - 1].astype(F32)
        place = half * lats + lat
        grad_ref[stream, core, place] = total.astype(grad_ref.dtype)
        mine = grad_ref.at[stream, core, place]
        copies = [
            send(mine, mine, stream * 6 + 3, turn - 1, turn - 1, lat_peer(turn)) for turn in order
        ]
        lon_copies, pair_copies = {}, []
        spread(stream, 0, lon_copies, pair_copies)
        return copies, lon_copies, pair_copies

    def start_spread(stream, started):
        copies, lon_copies, pair_copies = started
        for turn, copy in reversed(list(zip(order, copies))):
            copy.wait()
            spread(stream, turn, lon_copies, pair_copies)
        return lon_copies, pair_copies

    def start_pair_gather(stream, started):
        lon_copies, pair_copies = started
        for turn in [0] + order[::-1]:
            for step in range(1, halves):
                lon_copies[step, turn].wait()
                source = lax.rem(half + halves - step, halves)
                there = lax.rem(lat + lats - turn, lats)
                mine = grad_ref.at[stream, core, source * lats + there]
                slot = step * lats + turn
                pair_copies.append(send(mine, mine, stream * 6 + 5, slot, slot, pair))
        return pair_copies

    def pole_term(slot, start):
        return dot(wf[:, start : start + band], at_poles[slot], ((1,), (0,)))

    fill(0, accg, True)
    gen_copies = start_pair(0)
    open_gap = jnp.zeros((hid, (rows - 1) * width), F32)
    for step in range(steps):
        extra = None
        if step == 0:
            extra = jnp.concatenate([pole_term(0, 2 * band), open_gap], axis=1)
        elif step == steps - 1:
            extra = jnp.concatenate([open_gap, pole_term(1, 0)], axis=1)
        second_step(step, extra)
        if step == 1:
            gen_copies = start_lon(0, gen_copies)
    fill(1, accx, False)
    enc_copies = start_pair(1)

    for copy in hid_copies:
        copy.wait_send()
    for slot in range(2):
        arrive(hrow.at[slot * (height + 1)], 15, slot)

    def rebuild_step(step, packed):
        value = dot(wr[...], window(hrow, step * rows, 0, hid), ((1,), (0,)))
        for place in range(rows):
            row = step * rows + place
            lanes = slice(place * width, (place + 1) * width)
            left, centre, right = (value[tap * deep : (tap + 1) * deep, lanes] for tap in range(3))
            packed = packed + shifted(
                jnp.where(lane == width - 1, left, jnp.where(lane == 0, right, 0.0)), 2 * row + 1
            )
            inner = jnp.where(lane == 0, 0.0, shifted(left, 1))
            inner = inner + centre
            inner = inner + jnp.where(lane == width - 1, 0.0, shifted(right, -1))
            ysum[row] = inner
        return packed

    packed = jnp.zeros((deep, width), F32)
    packed = rebuild_step(0, packed)
    enc_copies = start_lon(1, enc_copies)
    gen_copies = start_lat(0, gen_copies)
    for step in range(1, steps):
        packed = rebuild_step(step, packed)
    ycol[...] = packed
    y_copies = [
        send(ycol, yhalo.at[0], 16, 0, 0, east),
        send(ycol, yhalo.at[1], 16, 1, 1, west),
    ]
    enc_copies = start_lat(1, enc_copies)

    def turn_out(load, target, size):
        for row in range(height):
            turned[pl.ds(row, size, stride=height), :] = load(row)
        target[...] = turned[: target.shape[0] * height].reshape(target.shape).astype(BF16)

    turn_out(lambda row: feat_rows[row].astype(F32), feat_ref, hid)
    gen_copies = start_lat_gather(0, gen_copies)
    for copy in y_copies:
        copy.wait()
    y_rims = jnp.where(lax.rem(lane, 2) == 0, shifted(yhalo[1], -1), shifted(yhalo[0], 1))

    def rebuilt_row(row):
        edges = shifted(y_rims, -(2 * row + 1))
        return ysum[row] + jnp.where((lane == 0) | (lane == width - 1), edges, 0.0)

    turn_out(rebuilt_row, reb_ref, deep)
    enc_copies = start_lat_gather(1, enc_copies)
    gen_copies = start_spread(0, gen_copies)
    gen_copies = start_pair_gather(0, gen_copies)
    enc_copies = start_spread(1, enc_copies)
    enc_copies = start_pair_gather(1, enc_copies)
    for copy in gen_copies + enc_copies:
        copy.wait()


def finish_kernel(norm, reb_in, feat_in, grad_in, reb_out, feat_out, enc_out, gen_out, flat, ready, sem):
    taps, count, hid = enc_out.shape
    side_lanes = hid // 2
    copies = [
        pltpu.make_async_copy(feat_in, feat_out, sem.at[0]),
        pltpu.make_async_copy(reb_in, reb_out, sem.at[1]),
    ]
    for copy in copies:
        copy.start()
    for stream, out in ((0, gen_out), (1, enc_out)):
        for side in range(2):
            gathered = grad_in[stream, side].astype(F32) * norm
            flat[:, side * side_lanes : (side + 1) * side_lanes] = gathered.reshape(-1, side_lanes)
        for tap in range(taps):
            ready[stream, tap] = flat[tap * count : (tap + 1) * count]
        copies.append(pltpu.make_async_copy(ready.at[stream], out, sem.at[2 + stream]))
        copies[-1].start()
    for copy in copies:
        copy.wait()


def on_device(fields, enc_kernel, gen_kernel, recon_grad):
    count, height, width = fields.shape
    hid = enc_kernel.shape[2]
    deep = -(-count // 16) * 16
    lats = lax.axis_size("lat")
    lons = lax.axis_size("lon")
    halves = lons // 2
    band = 3 * deep
    side_lanes = hid // 2
    chunks = halves * lats
    per = -(-9 * count // (chunks * 8)) * 8
    hops = (halves - 1) * lats
    counts = [halves, hops, lats - 1, lats - 1, hops, chunks] * 2 + [2, 4, 4, 2, 2]
    vmem = pl.BlockSpec(memory_space=pltpu.VMEM)
    anywhere = pl.BlockSpec(memory_space=pltpu.HBM)
    rebuilt, feat, summed = pl.pallas_call(
        functools.partial(layer_kernel, lats, halves, deep),
        out_shape=[
            jax.ShapeDtypeStruct((count, height, width), BF16),
            jax.ShapeDtypeStruct((hid, height, width), BF16),
            jax.ShapeDtypeStruct((2, 2, chunks, per, side_lanes), BF16),
        ],
        in_specs=[anywhere] * 4,
        out_specs=[vmem] * 3,
        scratch_shapes=[
            pltpu.VMEM((2, count, height, width), BF16),
            pltpu.VMEM((2, 9, count, hid), BF16),
            pltpu.VMEM((2, deep * height, width), F32),
            pltpu.VMEM((height + 2, 2 * band, width), BF16),
            pltpu.VMEM((deep // 2, width), BF16),
            pltpu.VMEM((2, deep // 2, width), BF16),
            pltpu.VMEM((2, 2, deep // 2, width), BF16),
            pltpu.VMEM((height + 2, hid, width), BF16),
            pltpu.VMEM((height // 4, hid, 4 * width), F32),
            pltpu.VMEM((height, hid, width), BF16),
            pltpu.VMEM((2, 9, deep, hid), BF16),
            pltpu.VMEM((hid, 9 * deep), BF16),
            pltpu.VMEM((hid, 9 * deep), BF16),
            pltpu.VMEM((band, 3 * hid), BF16),
            pltpu.VMEM((height, deep, width), F32),
            pltpu.VMEM((deep, width), F32),
            pltpu.VMEM((2, deep, width), F32),
            pltpu.VMEM((hid * height, width), F32),
            pltpu.VMEM((9 * deep, hid), F32),
            pltpu.VMEM((9 * deep, hid), F32),
            pltpu.VMEM((2, 2, chunks * per, side_lanes), F32),
            pltpu.VMEM((2, chunks * per, side_lanes), F32),
            pltpu.VMEM((2, chunks, per, side_lanes), LINK),
            pltpu.VMEM((2, halves - 1, lats, per, side_lanes), LINK),
            pltpu.VMEM((2, lats, per, side_lanes), LINK),
            pltpu.VMEM((2, lats - 1, per, side_lanes), LINK),
            pltpu.SemaphoreType.DMA((4,)),
        ]
        + [pltpu.SemaphoreType.DMA((size,)) for size in counts for _ in range(2)],
        compiler_params=pltpu.CompilerParams(
            collective_id=0, has_side_effects=True, vmem_limit_bytes=48 << 20
        ),
    )(
        *(pltpu.with_memory_space_constraint(v, pltpu.HBM) for v in (
        fields,
        recon_grad,
        enc_kernel.transpose(0, 1, 3, 2).reshape(9, count, hid),
        gen_kernel.reshape(9, count, hid),
        ))
    )
    norm = 1.0 / float(height * lats * width * lons) ** 0.5
    rebuilt, feat, enc_grad, gen_grad = pl.pallas_call(
        functools.partial(finish_kernel, norm),
        out_shape=[
            jax.ShapeDtypeStruct((count, height, width), BF16),
            jax.ShapeDtypeStruct((hid, height, width), BF16),
            jax.ShapeDtypeStruct((9, count, hid), F32),
            jax.ShapeDtypeStruct((9, count, hid), F32),
        ],
        in_specs=[vmem] * 3,
        out_specs=[anywhere] * 4,
        scratch_shapes=[
            pltpu.VMEM((chunks * per, hid), F32),
            pltpu.VMEM((2, 9, count, hid), F32),
            pltpu.SemaphoreType.DMA((4,)),
        ],
        compiler_params=pltpu.CompilerParams(vmem_limit_bytes=8 << 20),
    )(rebuilt, feat, summed)
    return (
        rebuilt,
        feat,
        enc_grad.reshape(3, 3, count, hid).transpose(0, 1, 3, 2),
        gen_grad.reshape(3, 3, count, hid),
    )


def solution(mesh):
    return jax.shard_map(
        on_device,
        mesh=mesh,
        in_specs=(P(None, "lat", "lon"), P(), P(), P(None, "lat", "lon")),
        out_specs=(P(None, "lat", "lon"), P(None, "lat", "lon"), P(), P()),
        check_vma=False,
    )
```

```python
import functools

import jax
import jax.numpy as jnp
from jax import lax
from jax.experimental import pallas as pl
from jax.experimental.pallas import tpu as pltpu
from jax.sharding import PartitionSpec as P

MESH = pl.DeviceIdType.MESH
LINK = jnp.bfloat16
F32 = jnp.float32
BF16 = jnp.bfloat16


def dot(left, right, dims):
    return lax.dot_general(left, right, (dims, ((), ())), preferred_element_type=F32)


def shifted(value, amount):
    width = value.shape[1]
    if isinstance(amount, int):
        amount = amount % width
        if amount == 0:
            return value
    return pltpu.roll(value, amount, 1)


def layer_kernel(
    lats, halves, deep, f_hbm, g_hbm, we_hbm, wg_hbm, reb_ref, feat_ref, grad_ref,
    fin, win, flat, xg, colp, colh, corner, hrow, dact, feat_rows, wpad, we, wf, wr,
    ysum, ycol, yhalo, turned, accx, accg, parts, from_pair, lon_out, from_lon, lat_out, from_lat, own,
    local_sem, greeted, *sems,
):
    count, height, width = fin.shape[1:]
    hid = hrow.shape[1]
    lons = 2 * halves
    band = 3 * deep
    half_deep = deep // 2
    lat = lax.axis_index("lat")
    lon = lax.axis_index("lon")
    half = lax.div(lon, 2)
    core = lax.rem(lon, 2)
    other = 1 - core
    below_top = lax.div(lat + lats - 1, lats)
    above_end = lax.div(2 * lats - 2 - lat, lats)

    def lon_peer(step):
        return (lat, lax.rem(half + step, halves) * 2 + core)

    def along(step):
        place = lat + step
        beyond = jnp.where((place < 0) | (place >= lats), 1, 0)
        mirrored = 2 * lats - 1 - place if step > 0 else -1 - place
        return (
            place + beyond * (mirrored - place),
            lax.rem(lon + beyond * halves, lons),
        )

    def greet(level):
        for step in (1 << level, -(1 << level)):
            pl.semaphore_signal(
                greeted.at[level], inc=1, device_id=along(step), device_id_type=MESH
            )

    def met(level):
        pl.semaphore_wait(greeted.at[level], 2)

    def north_of(place):
        return (lat - below_top, lax.rem(place + (1 - below_top) * halves, lons))

    def south_of(place):
        return (lat + above_end, lax.rem(place + (1 - above_end) * halves, lons))

    west_lon = lax.rem(lon + lons - 1, lons)
    east_lon = lax.rem(lon + 1, lons)
    pair = (lat, half * 2 + other)
    west = (lat, west_lon)
    east = (lat, east_lon)
    north = north_of(lon)
    south = south_of(lon)
    diagonals = [
        (south_of(east_lon), 1 - above_end, 0),
        (north_of(east_lon), below_top, 0),
        (south_of(west_lon), 1 - above_end, 1),
        (north_of(west_lon), below_top, 1),
    ]

    loads = [
        pltpu.make_async_copy(f_hbm, fin.at[0], local_sem.at[0]),
        pltpu.make_async_copy(g_hbm, fin.at[1], local_sem.at[1]),
        pltpu.make_async_copy(we_hbm, win.at[0], local_sem.at[2]),
        pltpu.make_async_copy(wg_hbm, win.at[1], local_sem.at[3]),
    ]
    for load in loads:
        load.start()

    barrier = pltpu.get_barrier_semaphore()
    peers = [west, east] + [peer for peer, slot, side in diagonals]
    peers += [lon_peer(step) for step in range(1, halves)]
    peers += [north, south]
    for peer in peers:
        pl.semaphore_signal(barrier, inc=1, device_id=peer, device_id_type=MESH)

    def send(src, dst, phase, send_slot, recv_slot, peer):
        copy = pltpu.make_async_remote_copy(
            src_ref=src,
            dst_ref=dst,
            send_sem=sems[2 * phase].at[send_slot],
            recv_sem=sems[2 * phase + 1].at[recv_slot],
            device_id=peer,
            device_id_type=MESH,
        )
        copy.start()
        return copy

    def arrive(ref, phase, slot):
        pltpu.make_async_copy(ref, ref, sems[2 * phase + 1].at[slot]).wait()

    def drain(ref, phase, slot):
        pltpu.make_async_copy(ref, ref, sems[2 * phase].at[slot]).wait()

    lane = lax.broadcasted_iota(jnp.int32, (deep, width), 1)
    half_lane = lax.broadcasted_iota(jnp.int32, (half_deep, width), 1)
    rim = (lane == 0) | (lane == width - 1)

    for array in range(2):
        for part in range(height // 8):
            flat[array, part, count * 8 :] = jnp.zeros(((deep - count) * 8, width), F32)
        wpad[array, :, deep - 16 :] = jnp.zeros((9, 16, hid), BF16)
    accx[...] = jnp.zeros_like(accx)
    accg[...] = jnp.zeros_like(accg)
    for load in loads[:2]:
        load.wait()
    for array in range(2):
        for part in range(height // 8):
            cells = fin[array, :, part * 8 : (part + 1) * 8].astype(F32)
            flat[array, part, : count * 8] = cells.reshape(count * 8, width)

    def cells_of(array, row):
        return flat[array, row // 8, pl.ds(row % 8, deep, stride=8), :]

    packed = jnp.zeros((half_deep, width), F32)
    for row in range(height):
        for array in range(2):
            cells = cells_of(array, row)
            xg[row + 1, array * band + deep : array * band + 2 * deep] = cells.astype(BF16)
            rims = jnp.where(rim, cells, 0.0)
            for part in range(2):
                packed = packed + shifted(
                    rims[part * half_deep : (part + 1) * half_deep],
                    2 * row + 1 + (2 * array + part) * 2 * height,
                )
    colp[...] = packed.astype(BF16)

    pl.semaphore_wait(barrier, len(peers))
    col_copies = [
        send(colp, colh.at[0], 12, 0, 0, east),
        send(colp, colh.at[1], 12, 1, 1, west),
    ]

    def send_rows(array):
        middle = pl.ds(array * band + deep, deep)
        return [
            send(
                xg.at[1, middle], xg.at[below_top * (height + 1), middle],
                13, 2 * array, 2 * array + below_top, north,
            ),
            send(
                xg.at[height, middle], xg.at[(1 - above_end) * (height + 1), middle],
                13, 2 * array + 1, 2 * array + 1 - above_end, south,
            ),
        ]

    row_copies = send_rows(0)
    corner_copies = [
        send(colp, corner.at[slot, side], 14, index, 2 * slot + side, peer)
        for index, (peer, slot, side) in enumerate(diagonals)
    ]
    row_copies += send_rows(1)
    levels = greeted.shape[0]
    greet(0)

    for load in loads[2:]:
        load.wait()
    for array in range(2):
        for tap in range(9):
            row_tap, col_tap = divmod(tap, 3)
            target = (2 - row_tap) * 3 + col_tap if array else tap
            wpad[array, target, :count] = win[array, tap]
    for tap in range(9):
        row_tap, col_tap = divmod(tap, 3)
        wr[col_tap * deep : (col_tap + 1) * deep, row_tap * hid : (row_tap + 1) * hid] = wpad[
            1, (2 - row_tap) * 3 + col_tap
        ]
    line = lax.broadcasted_iota(jnp.int32, (hid, hid), 0)
    column = lax.broadcasted_iota(jnp.int32, (hid, hid), 1)
    eye = jnp.where(line == column, 1.0, 0.0).astype(BF16)
    for array, target in ((0, we), (1, wf)):
        target[...] = dot(eye, wpad[array].reshape(9 * deep, hid), ((1,), (1,))).astype(BF16)

    even = lax.rem(half_lane, 2) == 0

    def join(from_west, from_east):
        return jnp.where(
            even, shifted(from_east.astype(F32), -1), shifted(from_west.astype(F32), 1)
        )

    def widen(array, slot, cells, rims, turn):
        parts_in = []
        for part in range(2):
            group = (2 * array + part) * 2 * height
            parts_in.append(shifted(rims, turn(group)))
        edges = jnp.concatenate(parts_in, axis=0)
        before = jnp.where(lane == 0, edges, shifted(cells, 1)).astype(BF16)
        after = jnp.where(lane == width - 1, edges, shifted(cells, -1)).astype(BF16)
        first, last = (after, before) if array else (before, after)
        base = array * band
        xg[slot, base : base + deep] = first
        xg[slot, base + 2 * deep : base + band] = last

    for copy in col_copies:
        copy.wait()
    own_rims = join(colh[0], colh[1])

    def centre_of(array, slot):
        return xg[slot, array * band + deep : array * band + 2 * deep].astype(F32)

    def widen_own(array):
        for row in range(height):
            widen(
                array, row + 1, centre_of(array, row + 1), own_rims,
                lambda group: -(2 * row + 1 + group),
            )

    widen_own(0)
    for copy in corner_copies:
        copy.wait_send()
    for slot in range(4):
        arrive(corner.at[slot // 2, slot % 2], 14, slot)
    for copy in row_copies:
        copy.wait_send()
    halo_rims = [join(corner[slot, 0], corner[slot, 1]) for slot in range(2)]
    source_rows = (below_top * (height - 1), (1 - above_end) * (height - 1))

    def widen_halo(array):
        middle = pl.ds(array * band + deep, deep)
        for slot in range(2):
            arrive(xg.at[slot * (height + 1), middle], 13, 2 * array + slot)
        for slot in range(2):
            cells = centre_of(array, slot * (height + 1))
            at = source_rows[slot]
            widen(
                array, slot * (height + 1), cells, halo_rims[slot],
                lambda group: lax.rem(2 * width - (2 * at + 1 + group), width),
            )

    widen_halo(0)
    widen_own(1)
    widen_halo(1)

    ends = ((0, below_top, 2 * band, 0), (1, above_end, 0, height - 1))
    met(0)
    if levels > 1:
        greet(1)
    at_poles = []
    for slot, inside, start, row in ends:
        edge = xg[slot * (height + 1), band:]
        at_poles.append(jnp.where(inside == 0, edge, jnp.zeros_like(edge)))
        xg[slot * (height + 1), band:] = jnp.where(inside == 0, jnp.zeros_like(edge), edge)

    rows = 4
    steps = height // rows

    def window(ref, row, start, size):
        return jnp.concatenate(
            [
                ref[pl.ds(row + place, 3), start : start + size].reshape(3 * size, width)
                for place in range(rows)
            ],
            axis=1,
        )

    def first_step(step):
        row = step * rows
        pre_act = dot(we[...], window(xg, row, 0, band), ((1,), (0,)))
        logistic = 1.0 / (1.0 + jnp.exp(-pre_act))
        gated = pre_act * logistic
        dact[step] = logistic + gated * (1.0 - logistic)
        hidden = gated.astype(BF16)
        for place in range(rows):
            hrow[row + 1 + place] = hidden[:, place * width : (place + 1) * width]
        accg[...] += dot(window(xg, row, band, band), hidden, ((1,), (1,)))

    def second_step(step, extra):
        row = step * rows
        feat = dot(wf[...], window(xg, row, band, band), ((1,), (0,)))
        if extra is not None:
            feat = feat + extra
        feat = feat.astype(BF16)
        for place in range(rows):
            feat_rows[row + place] = feat[:, place * width : (place + 1) * width]
        pre_grad = (feat.astype(F32) * dact[step]).astype(BF16)
        accx[...] += dot(window(xg, row, 0, band), pre_grad, ((1,), (1,)))

    for step in range(steps):
        first_step(step)
    for level in range(1, levels - 1):
        met(level)
        greet(level + 1)
    hid_copies = [
        send(hrow.at[1], hrow.at[below_top * (height + 1)], 15, 0, below_top, north),
        send(hrow.at[height], hrow.at[(1 - above_end) * (height + 1)], 15, 1, 1 - above_end, south),
    ]
    for slot, inside, start, row in ends:
        accg[start : start + band] += dot(at_poles[slot], hrow[row + 1], ((1,), (1,)))

    side_lanes = hid // 2
    per = lon_out.shape[2]
    owners = lat_out.shape[1]
    base = (lats - owners) // 2
    upper = lax.div(2 * lat, lats)
    owning = (lat >= base) & (lat < base + owners)
    for stream in range(2):
        from_lat[stream, lat] = jnp.zeros(from_lat.shape[2:], LINK)

    def fill(stream, acc, backward):
        used = 9 * count
        for tap in range(9):
            row_tap, col_tap = divmod(tap, 3)
            source = ((2 - row_tap) * 3 + col_tap if backward else tap) * deep
            for side in range(2):
                parts[stream, side, tap * count : (tap + 1) * count] = acc[
                    source : source + count, side * side_lanes : (side + 1) * side_lanes
                ]
        spare = parts.shape[2] - used
        if spare:
            for side in range(2):
                parts[stream, side, used:] = jnp.zeros((spare, side_lanes), F32)

    def piece(index, size):
        return pl.ds(pl.multiple_of(index * size, 8), size)

    def owner(index):
        return base + index + upper * (owners - 1 - 2 * index)

    def chunk_of(source, place):
        return source * owners + place

    def start_pair(stream):
        copies = {}
        for step in list(range(1, halves)) + [0]:
            part = piece(lax.rem(half + step, halves), owners * per)
            copies[step] = send(
                parts.at[stream, other, part], from_pair.at[stream, part], stream * 6, step, step, pair
            )
        return copies

    def start_lon(stream, copies):
        onward = {}
        for step in range(1, halves):
            copies[step].wait()
            target = lax.rem(half + step, halves)
            for index in reversed(range(owners)):
                place = owner(index) - base
                chunk = chunk_of(target, place)
                part = piece(chunk, per)
                lon_out[stream, chunk] = (
                    parts[stream, core, part] + from_pair[stream, part]
                ).astype(LINK)
                slot = (step - 1) * owners + index
                onward[step, index] = send(
                    lon_out.at[stream, chunk],
                    from_lon.at[stream, step - 1, place],
                    stream * 6 + 1, slot, slot, lon_peer(step),
                )
        copies[0].wait()
        return onward

    def start_lat(stream, copies):
        for index in reversed(range(owners)):
            to = owner(index)
            place = to - base
            part = piece(chunk_of(half, place), per)
            total = parts[stream, core, part] + from_pair[stream, part]
            for step in range(1, halves):
                copies[step, index].wait()
                total = total + from_lon[stream, step - 1, place].astype(F32)
            lat_out[stream, place] = total.astype(LINK)

            @pl.when(to == lat)
            def _():
                own[stream] = total

            @pl.when(to != lat)
            def _():
                send(
                    lat_out.at[stream, place], from_lat.at[stream, lat],
                    stream * 6 + 2, index, lat, (to, lon),
                )

    def spread(stream, place):
        mine = grad_ref.at[stream, core, chunk_of(half, place)]
        for step in range(1, halves):
            slot = (step - 1) * owners + place
            send(mine, mine, stream * 6 + 4, slot, slot, lon_peer(step))
        send(mine, mine, stream * 6 + 5, place, place, pair)

    def far_lat(index):
        rank = lats - 1 - index if index < lats // 2 else index - lats // 2
        return rank + upper * (lats - 1 - 2 * rank)

    def start_lat_gather(stream):
        @pl.when(owning)
        def _():
            for source in range(lats):

                @pl.when(source != lat)
                def _():
                    arrive(from_lat.at[stream, source], stream * 6 + 2, source)

            total = own[stream]
            for source in range(lats):
                total = total + from_lat[stream, source].astype(F32)
            place = lat - base
            chunk = chunk_of(half, place)
            grad_ref[stream, core, chunk] = total.astype(grad_ref.dtype)
            mine = grad_ref.at[stream, core, chunk]
            for index in range(lats):
                to = far_lat(index)

                @pl.when(to != lat)
                def _():
                    send(mine, mine, stream * 6 + 3, index, place, (to, lon))

            spread(stream, place)

    def start_spread(stream):
        for index in range(owners):
            place = owner(index) - base

            @pl.when(owner(index) != lat)
            def _():
                arrive(grad_ref.at[stream, core, chunk_of(half, place)], stream * 6 + 3, place)
                spread(stream, place)

    def start_pair_gather(stream):
        for index in range(owners):
            place = owner(index) - base
            for step in range(1, halves):
                source = lax.rem(half + halves - step, halves)
                mine = grad_ref.at[stream, core, chunk_of(source, place)]
                arrive(mine, stream * 6 + 4, (step - 1) * owners + place)
                slot = step * owners + place
                send(mine, mine, stream * 6 + 5, slot, slot, pair)

    def finish(stream):
        spare = lat_out.at[stream, 0]
        for place in range(owners):
            for step in range(halves):
                source = lax.rem(half + halves - step, halves)
                slot = step * owners + place
                arrive(grad_ref.at[stream, other, chunk_of(source, place)], stream * 6 + 5, slot)
                drain(spare, stream * 6 + 5, slot)
                if step:
                    drain(spare, stream * 6 + 4, (step - 1) * owners + place)

            @pl.when(owner(place) != lat)
            def _():
                drain(spare, stream * 6 + 2, place)

        @pl.when(owning)
        def _():
            for index in range(lats):

                @pl.when(far_lat(index) != lat)
                def _():
                    drain(spare, stream * 6 + 3, index)

    def pole_term(slot, start):
        return dot(wf[:, start : start + band], at_poles[slot], ((1,), (0,)))

    fill(0, accg, True)
    gen_copies = start_pair(0)
    open_gap = jnp.zeros((hid, (rows - 1) * width), F32)
    for step in range(steps):
        extra = None
        if step == 0:
            extra = jnp.concatenate([pole_term(0, 2 * band), open_gap], axis=1)
        elif step == steps - 1:
            extra = jnp.concatenate([open_gap, pole_term(1, 0)], axis=1)
        second_step(step, extra)
        if step == 1:
            gen_copies = start_lon(0, gen_copies)
    fill(1, accx, False)
    enc_copies = start_pair(1)

    for copy in hid_copies:
        copy.wait_send()
    for slot in range(2):
        arrive(hrow.at[slot * (height + 1)], 15, slot)

    def rebuild_step(step, packed):
        value = dot(wr[...], window(hrow, step * rows, 0, hid), ((1,), (0,)))
        for place in range(rows):
            row = step * rows + place
            lanes = slice(place * width, (place + 1) * width)
            left, centre, right = (value[tap * deep : (tap + 1) * deep, lanes] for tap in range(3))
            packed = packed + shifted(
                jnp.where(lane == width - 1, left, jnp.where(lane == 0, right, 0.0)), 2 * row + 1
            )
            inner = jnp.where(lane == 0, 0.0, shifted(left, 1))
            inner = inner + centre
            inner = inner + jnp.where(lane == width - 1, 0.0, shifted(right, -1))
            ysum[row] = inner
        return packed

    packed = jnp.zeros((deep, width), F32)
    enc_copies = start_lon(1, enc_copies)
    if levels > 1:
        met(levels - 1)
    start_lat(0, gen_copies)
    for step in range(steps):
        packed = rebuild_step(step, packed)
    ycol[...] = packed
    y_copies = [
        send(ycol, yhalo.at[0], 16, 0, 0, east),
        send(ycol, yhalo.at[1], 16, 1, 1, west),
    ]
    start_lat(1, enc_copies)

    def turn_out(load, target, size):
        for row in range(height):
            turned[row // 8, pl.ds(row % 8, size, stride=8), :] = load(row)
        kept = target.shape[0]
        target[...] = jnp.concatenate(
            [
                turned[part, : kept * 8].reshape(kept, 8, width)
                for part in range(height // 8)
            ],
            axis=1,
        ).astype(BF16)

    start_lat_gather(0)
    turn_out(lambda row: feat_rows[row].astype(F32), feat_ref, hid)
    for copy in y_copies:
        copy.wait()
    y_rims = jnp.where(lax.rem(lane, 2) == 0, shifted(yhalo[1], -1), shifted(yhalo[0], 1))

    def rebuilt_row(row):
        edges = shifted(y_rims, -(2 * row + 1))
        return ysum[row] + jnp.where((lane == 0) | (lane == width - 1), edges, 0.0)

    start_lat_gather(1)
    turn_out(rebuilt_row, reb_ref, deep)
    start_spread(0)
    start_pair_gather(0)
    start_spread(1)
    start_pair_gather(1)
    finish(0)
    finish(1)


def finish_kernel(norm, reb_in, feat_in, grad_in, reb_out, feat_out, enc_out, gen_out, flat, ready, sem):
    taps, count, hid = enc_out.shape
    side_lanes = hid // 2
    copies = [
        pltpu.make_async_copy(feat_in, feat_out, sem.at[0]),
        pltpu.make_async_copy(reb_in, reb_out, sem.at[1]),
    ]
    for copy in copies:
        copy.start()
    for stream, out in ((0, gen_out), (1, enc_out)):
        for side in range(2):
            gathered = grad_in[stream, side].astype(F32) * norm
            flat[:, side * side_lanes : (side + 1) * side_lanes] = gathered.reshape(-1, side_lanes)
        for tap in range(taps):
            ready[stream, tap] = flat[tap * count : (tap + 1) * count]
        copies.append(pltpu.make_async_copy(ready.at[stream], out, sem.at[2 + stream]))
        copies[-1].start()
    for copy in copies:
        copy.wait()


def on_device(fields, enc_kernel, gen_kernel, recon_grad):
    count, height, width = fields.shape
    hid = enc_kernel.shape[2]
    deep = -(-count // 16) * 16
    lats = lax.axis_size("lat")
    lons = lax.axis_size("lon")
    halves = lons // 2
    band = 3 * deep
    side_lanes = hid // 2
    owners = max(lats // 2, 1)
    chunks = halves * owners
    per = -(-9 * count // (chunks * 8)) * 8
    hops = (halves - 1) * owners
    levels = (lats - 1).bit_length()
    counts = [halves, hops, lats, lats, hops, chunks] * 2 + [2, 4, 4, 2, 2]
    vmem = pl.BlockSpec(memory_space=pltpu.VMEM)
    anywhere = pl.BlockSpec(memory_space=pltpu.HBM)
    rebuilt, feat, summed = pl.pallas_call(
        functools.partial(layer_kernel, lats, halves, deep),
        out_shape=[
            jax.ShapeDtypeStruct((count, height, width), BF16),
            jax.ShapeDtypeStruct((hid, height, width), BF16),
            jax.ShapeDtypeStruct((2, 2, chunks, per, side_lanes), BF16),
        ],
        in_specs=[anywhere] * 4,
        out_specs=[vmem] * 3,
        scratch_shapes=[
            pltpu.VMEM((2, count, height, width), BF16),
            pltpu.VMEM((2, 9, count, hid), BF16),
            pltpu.VMEM((2, height // 8, deep * 8, width), F32),
            pltpu.VMEM((height + 2, 2 * band, width), BF16),
            pltpu.VMEM((deep // 2, width), BF16),
            pltpu.VMEM((2, deep // 2, width), BF16),
            pltpu.VMEM((2, 2, deep // 2, width), BF16),
            pltpu.VMEM((height + 2, hid, width), BF16),
            pltpu.VMEM((height // 4, hid, 4 * width), F32),
            pltpu.VMEM((height, hid, width), BF16),
            pltpu.VMEM((2, 9, deep, hid), BF16),
            pltpu.VMEM((hid, 9 * deep), BF16),
            pltpu.VMEM((hid, 9 * deep), BF16),
            pltpu.VMEM((band, 3 * hid), BF16),
            pltpu.VMEM((height, deep, width), F32),
            pltpu.VMEM((deep, width), F32),
            pltpu.VMEM((2, deep, width), F32),
            pltpu.VMEM((height // 8, hid * 8, width), F32),
            pltpu.VMEM((9 * deep, hid), F32),
            pltpu.VMEM((9 * deep, hid), F32),
            pltpu.VMEM((2, 2, chunks * per, side_lanes), F32),
            pltpu.VMEM((2, chunks * per, side_lanes), F32),
            pltpu.VMEM((2, chunks, per, side_lanes), LINK),
            pltpu.VMEM((2, halves - 1, owners, per, side_lanes), LINK),
            pltpu.VMEM((2, owners, per, side_lanes), LINK),
            pltpu.VMEM((2, lats, per, side_lanes), LINK),
            pltpu.VMEM((2, per, side_lanes), F32),
            pltpu.SemaphoreType.DMA((4,)),
            pltpu.SemaphoreType.REGULAR((levels,)),
        ]
        + [pltpu.SemaphoreType.DMA((size,)) for size in counts for _ in range(2)],
        compiler_params=pltpu.CompilerParams(
            collective_id=0, has_side_effects=True, vmem_limit_bytes=48 << 20
        ),
    )(
        *(pltpu.with_memory_space_constraint(v, pltpu.HBM) for v in (
        fields,
        recon_grad,
        enc_kernel.transpose(0, 1, 3, 2).reshape(9, count, hid),
        gen_kernel.reshape(9, count, hid),
        ))
    )
    norm = 1.0 / float(height * lats * width * lons) ** 0.5
    rebuilt, feat, enc_grad, gen_grad = pl.pallas_call(
        functools.partial(finish_kernel, norm),
        out_shape=[
            jax.ShapeDtypeStruct((count, height, width), BF16),
            jax.ShapeDtypeStruct((hid, height, width), BF16),
            jax.ShapeDtypeStruct((9, count, hid), F32),
            jax.ShapeDtypeStruct((9, count, hid), F32),
        ],
        in_specs=[vmem] * 3,
        out_specs=[anywhere] * 4,
        scratch_shapes=[
            pltpu.VMEM((chunks * per, hid), F32),
            pltpu.VMEM((2, 9, count, hid), F32),
            pltpu.SemaphoreType.DMA((4,)),
        ],
        compiler_params=pltpu.CompilerParams(vmem_limit_bytes=8 << 20),
    )(rebuilt, feat, summed)
    return (
        rebuilt,
        feat,
        enc_grad.reshape(3, 3, count, hid).transpose(0, 1, 3, 2),
        gen_grad.reshape(3, 3, count, hid),
    )


def solution(mesh):
    return jax.shard_map(
        on_device,
        mesh=mesh,
        in_specs=(P(None, "lat", "lon"), P(), P(), P(None, "lat", "lon")),
        out_specs=(P(None, "lat", "lon"), P(None, "lat", "lon"), P(), P()),
        check_vma=False,
    )
```

```python
import functools

import jax
import jax.numpy as jnp
from jax import lax
from jax.experimental import pallas as pl
from jax.experimental.pallas import tpu as pltpu
from jax.sharding import PartitionSpec as P

MESH = pl.DeviceIdType.MESH
LINK = jnp.bfloat16
F32 = jnp.float32
BF16 = jnp.bfloat16


def dot(left, right, dims):
    return lax.dot_general(left, right, (dims, ((), ())), preferred_element_type=F32)


def shifted(value, amount):
    width = value.shape[1]
    if isinstance(amount, int):
        amount = amount % width
        if amount == 0:
            return value
    return pltpu.roll(value, amount, 1)


def layer_kernel(
    lats, halves, deep, f_hbm, g_hbm, we_hbm, wg_hbm, reb_ref, feat_ref, grad_ref,
    fin, win, flat, xg, colp, colh, corner, hrow, dact, feat_rows, wpad, we, wf, wr,
    ysum, ycol, yhalo, turned, accx, accg, parts, from_pair, lon_out, from_lon, lat_out, from_lat, own,
    local_sem, greeted, *sems,
):
    count, height, width = fin.shape[1:]
    hid = hrow.shape[1]
    lons = 2 * halves
    band = 3 * deep
    half_deep = deep // 2
    lat = lax.axis_index("lat")
    lon = lax.axis_index("lon")
    half = lax.div(lon, 2)
    core = lax.rem(lon, 2)
    other = 1 - core
    below_top = lax.div(lat + lats - 1, lats)
    above_end = lax.div(2 * lats - 2 - lat, lats)

    inner = lats // from_lat.shape[1]
    plane = halves * inner
    level_at = lax.div(lat, inner)
    row_at = lax.rem(lat, inner)

    def plane_peer(index):
        turn, swap = divmod(index, inner)
        return (
            level_at * inner + lax.rem(row_at + swap, inner),
            lax.rem(half + turn, halves) * 2 + core,
        )

    def along(step):
        place = lat + step
        beyond = jnp.where((place < 0) | (place >= lats), 1, 0)
        mirrored = 2 * lats - 1 - place if step > 0 else -1 - place
        return (
            place + beyond * (mirrored - place),
            lax.rem(lon + beyond * halves, lons),
        )

    def greet(level):
        for step in (1 << level, -(1 << level)):
            pl.semaphore_signal(
                greeted.at[level], inc=1, device_id=along(step), device_id_type=MESH
            )

    def met(level):
        pl.semaphore_wait(greeted.at[level], 2)

    def north_of(place):
        return (lat - below_top, lax.rem(place + (1 - below_top) * halves, lons))

    def south_of(place):
        return (lat + above_end, lax.rem(place + (1 - above_end) * halves, lons))

    west_lon = lax.rem(lon + lons - 1, lons)
    east_lon = lax.rem(lon + 1, lons)
    pair = (lat, half * 2 + other)
    west = (lat, west_lon)
    east = (lat, east_lon)
    north = north_of(lon)
    south = south_of(lon)
    diagonals = [
        (south_of(east_lon), 1 - above_end, 0),
        (north_of(east_lon), below_top, 0),
        (south_of(west_lon), 1 - above_end, 1),
        (north_of(west_lon), below_top, 1),
    ]

    loads = [
        pltpu.make_async_copy(f_hbm, fin.at[0], local_sem.at[0]),
        pltpu.make_async_copy(g_hbm, fin.at[1], local_sem.at[1]),
        pltpu.make_async_copy(we_hbm, win.at[0], local_sem.at[2]),
        pltpu.make_async_copy(wg_hbm, win.at[1], local_sem.at[3]),
    ]
    for load in loads:
        load.start()

    barrier = pltpu.get_barrier_semaphore()
    peers = [west, east] + [peer for peer, slot, side in diagonals]
    peers += [plane_peer(index) for index in range(1, plane)]
    peers += [north, south]
    for peer in peers:
        pl.semaphore_signal(barrier, inc=1, device_id=peer, device_id_type=MESH)

    def send(src, dst, phase, send_slot, recv_slot, peer):
        copy = pltpu.make_async_remote_copy(
            src_ref=src,
            dst_ref=dst,
            send_sem=sems[2 * phase].at[send_slot],
            recv_sem=sems[2 * phase + 1].at[recv_slot],
            device_id=peer,
            device_id_type=MESH,
        )
        copy.start()
        return copy

    def arrive(ref, phase, slot):
        pltpu.make_async_copy(ref, ref, sems[2 * phase + 1].at[slot]).wait()

    def drain(ref, phase, slot):
        pltpu.make_async_copy(ref, ref, sems[2 * phase].at[slot]).wait()

    lane = lax.broadcasted_iota(jnp.int32, (deep, width), 1)
    half_lane = lax.broadcasted_iota(jnp.int32, (half_deep, width), 1)
    rim = (lane == 0) | (lane == width - 1)

    for array in range(2):
        for part in range(height // 8):
            flat[array, part, count * 8 :] = jnp.zeros(((deep - count) * 8, width), F32)
        wpad[array, :, deep - 16 :] = jnp.zeros((9, 16, hid), BF16)
    accx[...] = jnp.zeros_like(accx)
    accg[...] = jnp.zeros_like(accg)
    for load in loads[:2]:
        load.wait()
    for array in range(2):
        for part in range(height // 8):
            cells = fin[array, :, part * 8 : (part + 1) * 8].astype(F32)
            flat[array, part, : count * 8] = cells.reshape(count * 8, width)

    def cells_of(array, row):
        return flat[array, row // 8, pl.ds(row % 8, deep, stride=8), :]

    packed = jnp.zeros((half_deep, width), F32)
    for row in range(height):
        for array in range(2):
            cells = cells_of(array, row)
            xg[row + 1, array * band + deep : array * band + 2 * deep] = cells.astype(BF16)
            rims = jnp.where(rim, cells, 0.0)
            for part in range(2):
                packed = packed + shifted(
                    rims[part * half_deep : (part + 1) * half_deep],
                    2 * row + 1 + (2 * array + part) * 2 * height,
                )
    colp[...] = packed.astype(BF16)

    pl.semaphore_wait(barrier, len(peers))
    col_copies = [
        send(colp, colh.at[0], 12, 0, 0, east),
        send(colp, colh.at[1], 12, 1, 1, west),
    ]

    def send_rows(array):
        middle = pl.ds(array * band + deep, deep)
        return [
            send(
                xg.at[1, middle], xg.at[below_top * (height + 1), middle],
                13, 2 * array, 2 * array + below_top, north,
            ),
            send(
                xg.at[height, middle], xg.at[(1 - above_end) * (height + 1), middle],
                13, 2 * array + 1, 2 * array + 1 - above_end, south,
            ),
        ]

    row_copies = send_rows(0)
    corner_copies = [
        send(colp, corner.at[slot, side], 14, index, 2 * slot + side, peer)
        for index, (peer, slot, side) in enumerate(diagonals)
    ]
    row_copies += send_rows(1)
    levels = greeted.shape[0]
    greet(0)

    for load in loads[2:]:
        load.wait()
    for array in range(2):
        for tap in range(9):
            row_tap, col_tap = divmod(tap, 3)
            target = (2 - row_tap) * 3 + col_tap if array else tap
            wpad[array, target, :count] = win[array, tap]
    for tap in range(9):
        row_tap, col_tap = divmod(tap, 3)
        wr[col_tap * deep : (col_tap + 1) * deep, row_tap * hid : (row_tap + 1) * hid] = wpad[
            1, (2 - row_tap) * 3 + col_tap
        ]
    line = lax.broadcasted_iota(jnp.int32, (hid, hid), 0)
    column = lax.broadcasted_iota(jnp.int32, (hid, hid), 1)
    eye = jnp.where(line == column, 1.0, 0.0).astype(BF16)
    for array, target in ((0, we), (1, wf)):
        target[...] = dot(eye, wpad[array].reshape(9 * deep, hid), ((1,), (1,))).astype(BF16)

    even = lax.rem(half_lane, 2) == 0

    def join(from_west, from_east):
        return jnp.where(
            even, shifted(from_east.astype(F32), -1), shifted(from_west.astype(F32), 1)
        )

    def widen(array, slot, cells, rims, turn):
        parts_in = []
        for part in range(2):
            group = (2 * array + part) * 2 * height
            parts_in.append(shifted(rims, turn(group)))
        edges = jnp.concatenate(parts_in, axis=0)
        before = jnp.where(lane == 0, edges, shifted(cells, 1)).astype(BF16)
        after = jnp.where(lane == width - 1, edges, shifted(cells, -1)).astype(BF16)
        first, last = (after, before) if array else (before, after)
        base = array * band
        xg[slot, base : base + deep] = first
        xg[slot, base + 2 * deep : base + band] = last

    for copy in col_copies:
        copy.wait()
    own_rims = join(colh[0], colh[1])

    def centre_of(array, slot):
        return xg[slot, array * band + deep : array * band + 2 * deep].astype(F32)

    def widen_own(array):
        for row in range(height):
            widen(
                array, row + 1, centre_of(array, row + 1), own_rims,
                lambda group: -(2 * row + 1 + group),
            )

    source_rows = (below_top * (height - 1), (1 - above_end) * (height - 1))

    def widen_halo(array, halo_rims):
        middle = pl.ds(array * band + deep, deep)
        for slot in range(2):
            arrive(xg.at[slot * (height + 1), middle], 13, 2 * array + slot)
        for slot in range(2):
            cells = centre_of(array, slot * (height + 1))
            at = source_rows[slot]
            widen(
                array, slot * (height + 1), cells, halo_rims[slot],
                lambda group: lax.rem(2 * width - (2 * at + 1 + group), width),
            )

    rows = 4
    steps = height // rows

    def window(ref, row, start, size):
        return jnp.concatenate(
            [
                ref[pl.ds(row + place, 3), start : start + size].reshape(3 * size, width)
                for place in range(rows)
            ],
            axis=1,
        )

    def conv_step(step):
        row = step * rows
        pre_act = dot(we[...], window(xg, row, 0, band), ((1,), (0,)))
        logistic = 1.0 / (1.0 + jnp.exp(-pre_act))
        gated = pre_act * logistic
        dact[step] = logistic + gated * (1.0 - logistic)
        hidden = gated.astype(BF16)
        for place in range(rows):
            hrow[row + 1 + place] = hidden[:, place * width : (place + 1) * width]

    def gen_step(step):
        row = step * rows
        hidden = jnp.concatenate([hrow[row + 1 + place] for place in range(rows)], axis=1)
        accg[...] += dot(window(xg, row, band, band), hidden, ((1,), (1,)))

    def second_step(step, extra):
        row = step * rows
        feat = dot(wf[...], window(xg, row, band, band), ((1,), (0,)))
        if extra is not None:
            feat = feat + extra
        feat = feat.astype(BF16)
        for place in range(rows):
            feat_rows[row + place] = feat[:, place * width : (place + 1) * width]
        pre_grad = (feat.astype(F32) * dact[step]).astype(BF16)
        accx[...] += dot(window(xg, row, 0, band), pre_grad, ((1,), (1,)))

    widen_own(0)
    met(0)
    if levels > 1:
        greet(1)
    for step in range(1, steps - 1):
        conv_step(step)
    widen_own(1)
    for copy in corner_copies:
        copy.wait_send()
    for slot in range(4):
        arrive(corner.at[slot // 2, slot % 2], 14, slot)
    for copy in row_copies:
        copy.wait_send()
    halo_rims = [join(corner[slot, 0], corner[slot, 1]) for slot in range(2)]
    widen_halo(0, halo_rims)
    for level in range(1, levels - 1):
        met(level)
        greet(level + 1)
    conv_step(0)
    conv_step(steps - 1)
    hid_copies = [
        send(hrow.at[1], hrow.at[below_top * (height + 1)], 15, 0, below_top, north),
        send(hrow.at[height], hrow.at[(1 - above_end) * (height + 1)], 15, 1, 1 - above_end, south),
    ]
    widen_halo(1, halo_rims)
    ends = ((0, below_top, 2 * band, 0), (1, above_end, 0, height - 1))
    at_poles = []
    for slot, inside, start, row in ends:
        edge = xg[slot * (height + 1), band:]
        at_poles.append(jnp.where(inside == 0, edge, jnp.zeros_like(edge)))
        xg[slot * (height + 1), band:] = jnp.where(inside == 0, jnp.zeros_like(edge), edge)
    for step in range(steps):
        gen_step(step)
    for slot, inside, start, row in ends:
        accg[start : start + band] += dot(at_poles[slot], hrow[row + 1], ((1,), (1,)))

    side_lanes = hid // 2
    per = lon_out.shape[2]
    owners = lat_out.shape[1]
    tall = from_lat.shape[1]
    base = (tall - owners) // 2
    upper = lax.div(2 * level_at, tall)
    owning = (level_at >= base) & (level_at < base + owners)
    for stream in range(2):
        from_lat[stream, level_at] = jnp.zeros(from_lat.shape[2:], LINK)

    def fill(stream, acc, backward):
        used = 9 * count
        for tap in range(9):
            row_tap, col_tap = divmod(tap, 3)
            source = ((2 - row_tap) * 3 + col_tap if backward else tap) * deep
            for side in range(2):
                parts[stream, side, tap * count : (tap + 1) * count] = acc[
                    source : source + count, side * side_lanes : (side + 1) * side_lanes
                ]
        spare = parts.shape[2] - used
        if spare:
            for side in range(2):
                parts[stream, side, used:] = jnp.zeros((spare, side_lanes), F32)

    def piece(index, size):
        return pl.ds(pl.multiple_of(index * size, 8), size)

    def owner(index):
        return base + index + upper * (owners - 1 - 2 * index)

    def block_of(index, forward):
        turn, swap = divmod(index, inner)
        source = lax.rem(half + (turn if forward else halves - turn), halves)
        return source * inner + lax.rem(row_at + swap, inner)

    def start_pair(stream):
        copies = {}
        for index in list(range(plane - 1, 0, -1)) + [0]:
            part = piece(block_of(index, True), owners * per)
            copies[index] = send(
                parts.at[stream, other, part], from_pair.at[stream, part],
                stream * 6, index, index, pair,
            )
        return copies

    def start_lon(stream, copies):
        onward = {}
        for index in range(plane - 1, 0, -1):
            copies[index].wait()
            for rank in reversed(range(owners)):
                place = owner(rank) - base
                chunk = block_of(index, True) * owners + place
                part = piece(chunk, per)
                lon_out[stream, chunk] = (
                    parts[stream, core, part] + from_pair[stream, part]
                ).astype(LINK)
                slot = (index - 1) * owners + rank
                onward[index, rank] = send(
                    lon_out.at[stream, chunk],
                    from_lon.at[stream, index - 1, place],
                    stream * 6 + 1, slot, slot, plane_peer(index),
                )
        copies[0].wait()
        return onward

    def start_lat(stream, copies):
        for rank in reversed(range(owners)):
            to = owner(rank)
            place = to - base
            part = piece(block_of(0, True) * owners + place, per)
            total = parts[stream, core, part] + from_pair[stream, part]
            for index in range(plane - 1, 0, -1):
                copies[index, rank].wait()
                total = total + from_lon[stream, index - 1, place].astype(F32)
            lat_out[stream, place] = total.astype(LINK)

            @pl.when(to == level_at)
            def _():
                own[stream] = total

            @pl.when(to != level_at)
            def _():
                send(
                    lat_out.at[stream, place], from_lat.at[stream, level_at],
                    stream * 6 + 2, rank, level_at, (to * inner + row_at, lon),
                )

    def spread(stream, place):
        mine = grad_ref.at[stream, core, block_of(0, True) * owners + place]
        for index in range(plane - 1, 0, -1):
            slot = (index - 1) * owners + place
            send(mine, mine, stream * 6 + 4, slot, slot, plane_peer(index))
        send(mine, mine, stream * 6 + 5, place, place, pair)

    def far_level(index):
        rank = tall - 1 - index if index < tall // 2 else index - tall // 2
        return rank + upper * (tall - 1 - 2 * rank)

    def start_lat_gather(stream):
        @pl.when(owning)
        def _():
            for source in range(tall):

                @pl.when(source != level_at)
                def _():
                    arrive(from_lat.at[stream, source], stream * 6 + 2, source)

            total = own[stream]
            for source in range(tall):
                total = total + from_lat[stream, source].astype(F32)
            place = level_at - base
            chunk = block_of(0, True) * owners + place
            grad_ref[stream, core, chunk] = total.astype(grad_ref.dtype)
            mine = grad_ref.at[stream, core, chunk]
            for index in range(tall):
                to = far_level(index)

                @pl.when(to != level_at)
                def _():
                    send(mine, mine, stream * 6 + 3, index, place, (to * inner + row_at, lon))

            spread(stream, place)

    def start_spread(stream):
        for rank in range(owners):
            place = owner(rank) - base

            @pl.when(owner(rank) != level_at)
            def _():
                chunk = block_of(0, True) * owners + place
                arrive(grad_ref.at[stream, core, chunk], stream * 6 + 3, place)
                spread(stream, place)

    def start_pair_gather(stream):
        for rank in range(owners):
            place = owner(rank) - base
            for index in range(1, plane):
                mine = grad_ref.at[stream, core, block_of(index, False) * owners + place]
                arrive(mine, stream * 6 + 4, (index - 1) * owners + place)
                slot = index * owners + place
                send(mine, mine, stream * 6 + 5, slot, slot, pair)

    def finish(stream):
        spare = lat_out.at[stream, 0]
        for place in range(owners):
            for index in range(plane):
                chunk = block_of(index, False) * owners + place
                slot = index * owners + place
                arrive(grad_ref.at[stream, other, chunk], stream * 6 + 5, slot)
                drain(spare, stream * 6 + 5, slot)
                if index:
                    drain(spare, stream * 6 + 4, (index - 1) * owners + place)

            @pl.when(owner(place) != level_at)
            def _():
                drain(spare, stream * 6 + 2, place)

        @pl.when(owning)
        def _():
            for index in range(tall):

                @pl.when(far_level(index) != level_at)
                def _():
                    drain(spare, stream * 6 + 3, index)

    def pole_term(slot, start):
        return dot(wf[:, start : start + band], at_poles[slot], ((1,), (0,)))

    fill(0, accg, True)
    gen_copies = start_pair(0)
    open_gap = jnp.zeros((hid, (rows - 1) * width), F32)
    for step in range(steps):
        extra = None
        if step == 0:
            extra = jnp.concatenate([pole_term(0, 2 * band), open_gap], axis=1)
        elif step == steps - 1:
            extra = jnp.concatenate([open_gap, pole_term(1, 0)], axis=1)
        second_step(step, extra)
        if step == 1:
            gen_copies = start_lon(0, gen_copies)
    fill(1, accx, False)
    enc_copies = start_pair(1)

    for copy in hid_copies:
        copy.wait_send()
    for slot in range(2):
        arrive(hrow.at[slot * (height + 1)], 15, slot)

    def rebuild_step(step, packed):
        value = dot(wr[...], window(hrow, step * rows, 0, hid), ((1,), (0,)))
        for place in range(rows):
            row = step * rows + place
            lanes = slice(place * width, (place + 1) * width)
            left, centre, right = (value[tap * deep : (tap + 1) * deep, lanes] for tap in range(3))
            packed = packed + shifted(
                jnp.where(lane == width - 1, left, jnp.where(lane == 0, right, 0.0)), 2 * row + 1
            )
            inner = jnp.where(lane == 0, 0.0, shifted(left, 1))
            inner = inner + centre
            inner = inner + jnp.where(lane == width - 1, 0.0, shifted(right, -1))
            ysum[row] = inner
        return packed

    packed = jnp.zeros((deep, width), F32)
    enc_copies = start_lon(1, enc_copies)
    if levels > 1:
        met(levels - 1)
    start_lat(0, gen_copies)
    for step in range(steps):
        packed = rebuild_step(step, packed)
    ycol[...] = packed
    y_copies = [
        send(ycol, yhalo.at[0], 16, 0, 0, east),
        send(ycol, yhalo.at[1], 16, 1, 1, west),
    ]
    start_lat(1, enc_copies)

    def turn_out(load, target, size):
        for row in range(height):
            turned[row // 8, pl.ds(row % 8, size, stride=8), :] = load(row)
        kept = target.shape[0]
        target[...] = jnp.concatenate(
            [
                turned[part, : kept * 8].reshape(kept, 8, width)
                for part in range(height // 8)
            ],
            axis=1,
        ).astype(BF16)

    start_lat_gather(0)
    turn_out(lambda row: feat_rows[row].astype(F32), feat_ref, hid)
    for copy in y_copies:
        copy.wait()
    y_rims = jnp.where(lax.rem(lane, 2) == 0, shifted(yhalo[1], -1), shifted(yhalo[0], 1))

    def rebuilt_row(row):
        edges = shifted(y_rims, -(2 * row + 1))
        return ysum[row] + jnp.where((lane == 0) | (lane == width - 1), edges, 0.0)

    start_lat_gather(1)
    turn_out(rebuilt_row, reb_ref, deep)
    start_spread(0)
    start_spread(1)
    start_pair_gather(0)
    start_pair_gather(1)
    finish(0)
    finish(1)


def finish_kernel(norm, reb_in, feat_in, grad_in, reb_out, feat_out, enc_out, gen_out, flat, ready, sem):
    taps, count, hid = enc_out.shape
    side_lanes = hid // 2
    copies = [
        pltpu.make_async_copy(feat_in, feat_out, sem.at[0]),
        pltpu.make_async_copy(reb_in, reb_out, sem.at[1]),
    ]
    for copy in copies:
        copy.start()
    for stream, out in ((0, gen_out), (1, enc_out)):
        for side in range(2):
            gathered = grad_in[stream, side].astype(F32) * norm
            flat[:, side * side_lanes : (side + 1) * side_lanes] = gathered.reshape(-1, side_lanes)
        for tap in range(taps):
            ready[stream, tap] = flat[tap * count : (tap + 1) * count]
        copies.append(pltpu.make_async_copy(ready.at[stream], out, sem.at[2 + stream]))
        copies[-1].start()
    for copy in copies:
        copy.wait()


def on_device(fields, enc_kernel, gen_kernel, recon_grad):
    count, height, width = fields.shape
    hid = enc_kernel.shape[2]
    deep = -(-count // 16) * 16
    lats = lax.axis_size("lat")
    lons = lax.axis_size("lon")
    halves = lons // 2
    band = 3 * deep
    side_lanes = hid // 2
    inner = 2
    tall = lats // inner
    owners = tall // 2
    plane = halves * inner
    chunks = plane * owners
    per = -(-9 * count // (chunks * 8)) * 8
    hops = (plane - 1) * owners
    reach = inner * (tall - 1 - (tall - owners) // 2)
    levels = (reach - 1).bit_length()
    counts = [plane, hops, tall, tall, hops, chunks] * 2 + [2, 4, 4, 2, 2]
    vmem = pl.BlockSpec(memory_space=pltpu.VMEM)
    anywhere = pl.BlockSpec(memory_space=pltpu.HBM)
    rebuilt, feat, summed = pl.pallas_call(
        functools.partial(layer_kernel, lats, halves, deep),
        out_shape=[
            jax.ShapeDtypeStruct((count, height, width), BF16),
            jax.ShapeDtypeStruct((hid, height, width), BF16),
            jax.ShapeDtypeStruct((2, 2, chunks, per, side_lanes), BF16),
        ],
        in_specs=[anywhere] * 4,
        out_specs=[vmem] * 3,
        scratch_shapes=[
            pltpu.VMEM((2, count, height, width), BF16),
            pltpu.VMEM((2, 9, count, hid), BF16),
            pltpu.VMEM((2, height // 8, deep * 8, width), F32),
            pltpu.VMEM((height + 2, 2 * band, width), BF16),
            pltpu.VMEM((deep // 2, width), BF16),
            pltpu.VMEM((2, deep // 2, width), BF16),
            pltpu.VMEM((2, 2, deep // 2, width), BF16),
            pltpu.VMEM((height + 2, hid, width), BF16),
            pltpu.VMEM((height // 4, hid, 4 * width), F32),
            pltpu.VMEM((height, hid, width), BF16),
            pltpu.VMEM((2, 9, deep, hid), BF16),
            pltpu.VMEM((hid, 9 * deep), BF16),
            pltpu.VMEM((hid, 9 * deep), BF16),
            pltpu.VMEM((band, 3 * hid), BF16),
            pltpu.VMEM((height, deep, width), F32),
            pltpu.VMEM((deep, width), F32),
            pltpu.VMEM((2, deep, width), F32),
            pltpu.VMEM((height // 8, hid * 8, width), F32),
            pltpu.VMEM((9 * deep, hid), F32),
            pltpu.VMEM((9 * deep, hid), F32),
            pltpu.VMEM((2, 2, chunks * per, side_lanes), F32),
            pltpu.VMEM((2, chunks * per, side_lanes), F32),
            pltpu.VMEM((2, chunks, per, side_lanes), LINK),
            pltpu.VMEM((2, plane - 1, owners, per, side_lanes), LINK),
            pltpu.VMEM((2, owners, per, side_lanes), LINK),
            pltpu.VMEM((2, tall, per, side_lanes), LINK),
            pltpu.VMEM((2, per, side_lanes), F32),
            pltpu.SemaphoreType.DMA((4,)),
            pltpu.SemaphoreType.REGULAR((levels,)),
        ]
        + [pltpu.SemaphoreType.DMA((size,)) for size in counts for _ in range(2)],
        compiler_params=pltpu.CompilerParams(
            collective_id=0, has_side_effects=True, vmem_limit_bytes=48 << 20
        ),
    )(
        *(pltpu.with_memory_space_constraint(v, pltpu.HBM) for v in (
        fields,
        recon_grad,
        enc_kernel.transpose(0, 1, 3, 2).reshape(9, count, hid),
        gen_kernel.reshape(9, count, hid),
        ))
    )
    norm = 1.0 / float(height * lats * width * lons) ** 0.5
    rebuilt, feat, enc_grad, gen_grad = pl.pallas_call(
        functools.partial(finish_kernel, norm),
        out_shape=[
            jax.ShapeDtypeStruct((count, height, width), BF16),
            jax.ShapeDtypeStruct((hid, height, width), BF16),
            jax.ShapeDtypeStruct((9, count, hid), F32),
            jax.ShapeDtypeStruct((9, count, hid), F32),
        ],
        in_specs=[vmem] * 3,
        out_specs=[anywhere] * 4,
        scratch_shapes=[
            pltpu.VMEM((chunks * per, hid), F32),
            pltpu.VMEM((2, 9, count, hid), F32),
            pltpu.SemaphoreType.DMA((4,)),
        ],
        compiler_params=pltpu.CompilerParams(vmem_limit_bytes=8 << 20),
    )(rebuilt, feat, summed)
    return (
        rebuilt,
        feat,
        enc_grad.reshape(3, 3, count, hid).transpose(0, 1, 3, 2),
        gen_grad.reshape(3, 3, count, hid),
    )


def solution(mesh):
    return jax.shard_map(
        on_device,
        mesh=mesh,
        in_specs=(P(None, "lat", "lon"), P(), P(), P(None, "lat", "lon")),
        out_specs=(P(None, "lat", "lon"), P(None, "lat", "lon"), P(), P()),
        check_vma=False,
    )
```

```python
import functools

import jax
import jax.numpy as jnp
from jax import lax
from jax.experimental import pallas as pl
from jax.experimental.pallas import tpu as pltpu
from jax.sharding import PartitionSpec as P

MESH = pl.DeviceIdType.MESH
LINK = jnp.bfloat16
F32 = jnp.float32
BF16 = jnp.bfloat16


def dot(left, right, dims):
    return lax.dot_general(left, right, (dims, ((), ())), preferred_element_type=F32)


def shifted(value, amount):
    width = value.shape[1]
    if isinstance(amount, int):
        amount = amount % width
        if amount == 0:
            return value
    return pltpu.roll(value, amount, 1)


def layer_kernel(
    lats, halves, deep, f_hbm, g_hbm, we_hbm, wg_hbm, reb_ref, feat_ref, grad_ref,
    fin, win, flat, xg, colp, colh, corner, hrow, dact, feat_rows, wpad, we, wf, wr,
    ysum, ycol, yhalo, turned, accx, accg, parts, from_pair, lon_out, from_lon, lat_out, from_lat, own,
    local_sem, greeted, *sems,
):
    count, height, width = fin.shape[1:]
    hid = hrow.shape[1]
    lons = 2 * halves
    band = 3 * deep
    half_deep = deep // 2
    lat = lax.axis_index("lat")
    lon = lax.axis_index("lon")
    half = lax.div(lon, 2)
    core = lax.rem(lon, 2)
    other = 1 - core
    below_top = lax.div(lat + lats - 1, lats)
    above_end = lax.div(2 * lats - 2 - lat, lats)

    inner = lats // from_lat.shape[1]
    plane = halves * inner
    level_at = lax.div(lat, inner)
    row_at = lax.rem(lat, inner)

    def plane_peer(index):
        turn, swap = divmod(index, inner)
        return (
            level_at * inner + lax.rem(row_at + swap, inner),
            lax.rem(half + turn, halves) * 2 + core,
        )

    def along(step):
        place = lat + step
        beyond = jnp.where((place < 0) | (place >= lats), 1, 0)
        mirrored = 2 * lats - 1 - place if step > 0 else -1 - place
        return (
            place + beyond * (mirrored - place),
            lax.rem(lon + beyond * halves, lons),
        )

    def greet(level):
        for step in (1 << level, -(1 << level)):
            pl.semaphore_signal(
                greeted.at[level], inc=1, device_id=along(step), device_id_type=MESH
            )

    def met(level):
        pl.semaphore_wait(greeted.at[level], 2)

    def north_of(place):
        return (lat - below_top, lax.rem(place + (1 - below_top) * halves, lons))

    def south_of(place):
        return (lat + above_end, lax.rem(place + (1 - above_end) * halves, lons))

    west_lon = lax.rem(lon + lons - 1, lons)
    east_lon = lax.rem(lon + 1, lons)
    pair = (lat, half * 2 + other)
    west = (lat, west_lon)
    east = (lat, east_lon)
    north = north_of(lon)
    south = south_of(lon)
    diagonals = [
        (south_of(east_lon), 1 - above_end, 0),
        (north_of(east_lon), below_top, 0),
        (south_of(west_lon), 1 - above_end, 1),
        (north_of(west_lon), below_top, 1),
    ]

    loads = [
        pltpu.make_async_copy(f_hbm, fin.at[0], local_sem.at[0]),
        pltpu.make_async_copy(g_hbm, fin.at[1], local_sem.at[1]),
        pltpu.make_async_copy(we_hbm, win.at[0], local_sem.at[2]),
        pltpu.make_async_copy(wg_hbm, win.at[1], local_sem.at[3]),
    ]
    for load in loads:
        load.start()

    barrier = pltpu.get_barrier_semaphore()
    peers = [west, east] + [peer for peer, slot, side in diagonals]
    peers += [plane_peer(index) for index in range(1, plane)]
    peers += [north, south]
    for peer in peers:
        pl.semaphore_signal(barrier, inc=1, device_id=peer, device_id_type=MESH)

    def send(src, dst, phase, send_slot, recv_slot, peer):
        copy = pltpu.make_async_remote_copy(
            src_ref=src,
            dst_ref=dst,
            send_sem=sems[2 * phase].at[send_slot],
            recv_sem=sems[2 * phase + 1].at[recv_slot],
            device_id=peer,
            device_id_type=MESH,
        )
        copy.start()
        return copy

    def arrive(ref, phase, slot):
        pltpu.make_async_copy(ref, ref, sems[2 * phase + 1].at[slot]).wait()

    def drain(ref, phase, slot):
        pltpu.make_async_copy(ref, ref, sems[2 * phase].at[slot]).wait()

    lane = lax.broadcasted_iota(jnp.int32, (deep, width), 1)
    half_lane = lax.broadcasted_iota(jnp.int32, (half_deep, width), 1)
    rim = (lane == 0) | (lane == width - 1)

    for array in range(2):
        for part in range(height // 8):
            flat[array, part, count * 8 :] = jnp.zeros(((deep - count) * 8, width), F32)
        wpad[array, :, deep - 16 :] = jnp.zeros((9, 16, hid), BF16)
    accx[...] = jnp.zeros_like(accx)
    accg[...] = jnp.zeros_like(accg)
    for load in loads[:2]:
        load.wait()
    for array in range(2):
        for part in range(height // 8):
            cells = fin[array, :, part * 8 : (part + 1) * 8].astype(F32)
            flat[array, part, : count * 8] = cells.reshape(count * 8, width)

    def cells_of(array, row):
        return flat[array, row // 8, pl.ds(row % 8, deep, stride=8), :]

    packed = jnp.zeros((half_deep, width), F32)
    for row in range(height):
        for array in range(2):
            cells = cells_of(array, row)
            xg[row + 1, array * band + deep : array * band + 2 * deep] = cells.astype(BF16)
            rims = jnp.where(rim, cells, 0.0)
            for part in range(2):
                packed = packed + shifted(
                    rims[part * half_deep : (part + 1) * half_deep],
                    2 * row + 1 + (2 * array + part) * 2 * height,
                )
    colp[...] = packed.astype(BF16)

    pl.semaphore_wait(barrier, len(peers))
    col_copies = [
        send(colp, colh.at[0], 12, 0, 0, east),
        send(colp, colh.at[1], 12, 1, 1, west),
    ]

    def send_rows(array):
        middle = pl.ds(array * band + deep, deep)
        return [
            send(
                xg.at[1, middle], xg.at[below_top * (height + 1), middle],
                13, 2 * array, 2 * array + below_top, north,
            ),
            send(
                xg.at[height, middle], xg.at[(1 - above_end) * (height + 1), middle],
                13, 2 * array + 1, 2 * array + 1 - above_end, south,
            ),
        ]

    row_copies = send_rows(0)
    corner_copies = [
        send(colp, corner.at[slot, side], 14, index, 2 * slot + side, peer)
        for index, (peer, slot, side) in enumerate(diagonals)
    ]
    row_copies += send_rows(1)
    levels = greeted.shape[0]
    greet(0)

    for load in loads[2:]:
        load.wait()
    for array in range(2):
        for tap in range(9):
            row_tap, col_tap = divmod(tap, 3)
            target = (2 - row_tap) * 3 + col_tap if array else tap
            wpad[array, target, :count] = win[array, tap]
    for tap in range(9):
        row_tap, col_tap = divmod(tap, 3)
        wr[col_tap * deep : (col_tap + 1) * deep, row_tap * hid : (row_tap + 1) * hid] = wpad[
            1, (2 - row_tap) * 3 + col_tap
        ]
    line = lax.broadcasted_iota(jnp.int32, (hid, hid), 0)
    column = lax.broadcasted_iota(jnp.int32, (hid, hid), 1)
    eye = jnp.where(line == column, 1.0, 0.0).astype(BF16)
    for array, target in ((0, we), (1, wf)):
        target[...] = dot(eye, wpad[array].reshape(9 * deep, hid), ((1,), (1,))).astype(BF16)

    even = lax.rem(half_lane, 2) == 0

    def join(from_west, from_east):
        return jnp.where(
            even, shifted(from_east.astype(F32), -1), shifted(from_west.astype(F32), 1)
        )

    def widen(array, slot, cells, rims, turn):
        parts_in = []
        for part in range(2):
            group = (2 * array + part) * 2 * height
            parts_in.append(shifted(rims, turn(group)))
        edges = jnp.concatenate(parts_in, axis=0)
        before = jnp.where(lane == 0, edges, shifted(cells, 1)).astype(BF16)
        after = jnp.where(lane == width - 1, edges, shifted(cells, -1)).astype(BF16)
        first, last = (after, before) if array else (before, after)
        base = array * band
        xg[slot, base : base + deep] = first
        xg[slot, base + 2 * deep : base + band] = last

    for copy in col_copies:
        copy.wait()
    own_rims = join(colh[0], colh[1])

    def centre_of(array, slot):
        return xg[slot, array * band + deep : array * band + 2 * deep].astype(F32)

    def widen_own(array):
        for row in range(height):
            widen(
                array, row + 1, centre_of(array, row + 1), own_rims,
                lambda group: -(2 * row + 1 + group),
            )

    source_rows = (below_top * (height - 1), (1 - above_end) * (height - 1))

    def widen_halo(array, halo_rims):
        middle = pl.ds(array * band + deep, deep)
        for slot in range(2):
            arrive(xg.at[slot * (height + 1), middle], 13, 2 * array + slot)
        for slot in range(2):
            cells = centre_of(array, slot * (height + 1))
            at = source_rows[slot]
            widen(
                array, slot * (height + 1), cells, halo_rims[slot],
                lambda group: lax.rem(2 * width - (2 * at + 1 + group), width),
            )

    rows = 4
    steps = height // rows

    def window(ref, row, start, size):
        return jnp.concatenate(
            [
                ref[pl.ds(row + place, 3), start : start + size].reshape(3 * size, width)
                for place in range(rows)
            ],
            axis=1,
        )

    def conv_step(step):
        row = step * rows
        pre_act = dot(we[...], window(xg, row, 0, band), ((1,), (0,)))
        logistic = 1.0 / (1.0 + jnp.exp(-pre_act))
        gated = pre_act * logistic
        dact[step] = logistic + gated * (1.0 - logistic)
        hidden = gated.astype(BF16)
        for place in range(rows):
            hrow[row + 1 + place] = hidden[:, place * width : (place + 1) * width]

    def gen_step(step):
        row = step * rows
        hidden = jnp.concatenate([hrow[row + 1 + place] for place in range(rows)], axis=1)
        accg[...] += dot(window(xg, row, band, band), hidden, ((1,), (1,)))

    def second_step(step, extra):
        row = step * rows
        feat = dot(wf[...], window(xg, row, band, band), ((1,), (0,)))
        if extra is not None:
            feat = feat + extra
        feat = feat.astype(BF16)
        for place in range(rows):
            feat_rows[row + place] = feat[:, place * width : (place + 1) * width]
        pre_grad = (feat.astype(F32) * dact[step]).astype(BF16)
        accx[...] += dot(window(xg, row, 0, band), pre_grad, ((1,), (1,)))

    widen_own(0)
    met(0)
    if levels > 1:
        greet(1)
    for step in range(1, steps - 1):
        conv_step(step)
    widen_own(1)
    for copy in corner_copies:
        copy.wait_send()
    for slot in range(4):
        arrive(corner.at[slot // 2, slot % 2], 14, slot)
    for copy in row_copies:
        copy.wait_send()
    halo_rims = [join(corner[slot, 0], corner[slot, 1]) for slot in range(2)]
    widen_halo(0, halo_rims)
    for level in range(1, levels - 1):
        met(level)
        greet(level + 1)
    conv_step(0)
    conv_step(steps - 1)
    hid_copies = [
        send(hrow.at[1], hrow.at[below_top * (height + 1)], 15, 0, below_top, north),
        send(hrow.at[height], hrow.at[(1 - above_end) * (height + 1)], 15, 1, 1 - above_end, south),
    ]
    widen_halo(1, halo_rims)
    ends = ((0, below_top, 2 * band, 0), (1, above_end, 0, height - 1))
    at_poles = []
    for slot, inside, start, row in ends:
        edge = xg[slot * (height + 1), band:]
        at_poles.append(jnp.where(inside == 0, edge, jnp.zeros_like(edge)))
        xg[slot * (height + 1), band:] = jnp.where(inside == 0, jnp.zeros_like(edge), edge)
    for step in range(steps):
        gen_step(step)
    for slot, inside, start, row in ends:
        accg[start : start + band] += dot(at_poles[slot], hrow[row + 1], ((1,), (1,)))

    side_lanes = hid // 2
    per = lon_out.shape[2]
    owners = lat_out.shape[1]
    tall = from_lat.shape[1]
    base = (tall - owners) // 2
    upper = lax.div(2 * level_at, tall)
    owning = (level_at >= base) & (level_at < base + owners)
    for stream in range(2):
        from_lat[stream, level_at] = jnp.zeros(from_lat.shape[2:], LINK)

    def fill(stream, acc, backward):
        used = 9 * count
        for tap in range(9):
            row_tap, col_tap = divmod(tap, 3)
            source = ((2 - row_tap) * 3 + col_tap if backward else tap) * deep
            for side in range(2):
                parts[stream, side, tap * count : (tap + 1) * count] = acc[
                    source : source + count, side * side_lanes : (side + 1) * side_lanes
                ]
        spare = parts.shape[2] - used
        if spare:
            for side in range(2):
                parts[stream, side, used:] = jnp.zeros((spare, side_lanes), F32)

    def piece(index, size):
        return pl.ds(pl.multiple_of(index * size, 8), size)

    def owner(index):
        return base + index + upper * (owners - 1 - 2 * index)

    def block_of(index, forward):
        turn, swap = divmod(index, inner)
        source = lax.rem(half + (turn if forward else halves - turn), halves)
        return source * inner + lax.rem(row_at + swap, inner)

    def start_pair(stream):
        copies = {}
        for index in list(range(plane - 1, 0, -1)) + [0]:
            part = piece(block_of(index, True), owners * per)
            copies[index] = send(
                parts.at[stream, other, part], from_pair.at[stream, part],
                stream * 6, index, index, pair,
            )
        return copies

    def start_lon(stream, copies):
        onward = {}
        for index in range(plane - 1, 0, -1):
            copies[index].wait()
            for rank in reversed(range(owners)):
                place = owner(rank) - base
                chunk = block_of(index, True) * owners + place
                part = piece(chunk, per)
                lon_out[stream, chunk] = (
                    parts[stream, core, part] + from_pair[stream, part]
                ).astype(LINK)
                slot = (index - 1) * owners + rank
                onward[index, rank] = send(
                    lon_out.at[stream, chunk],
                    from_lon.at[stream, index - 1, place],
                    stream * 6 + 1, slot, slot, plane_peer(index),
                )
        copies[0].wait()
        return onward

    def start_lat(stream, copies):
        for rank in reversed(range(owners)):
            to = owner(rank)
            place = to - base
            part = piece(block_of(0, True) * owners + place, per)
            total = parts[stream, core, part] + from_pair[stream, part]
            for index in range(plane - 1, 0, -1):
                copies[index, rank].wait()
                total = total + from_lon[stream, index - 1, place].astype(F32)
            lat_out[stream, place] = total.astype(LINK)

            @pl.when(to == level_at)
            def _():
                own[stream] = total

            @pl.when(to != level_at)
            def _():
                send(
                    lat_out.at[stream, place], from_lat.at[stream, level_at],
                    stream * 6 + 2, rank, level_at, (to * inner + row_at, lon),
                )

    def spread(stream, place):
        mine = grad_ref.at[stream, core, block_of(0, True) * owners + place]
        for index in range(plane - 1, 0, -1):
            slot = (index - 1) * owners + place
            send(mine, mine, stream * 6 + 4, slot, slot, plane_peer(index))
        send(mine, mine, stream * 6 + 5, place, place, pair)

    def far_level(index):
        rank = tall - 1 - index if index < tall // 2 else index - tall // 2
        return rank + upper * (tall - 1 - 2 * rank)

    def start_lat_gather(stream):
        @pl.when(owning)
        def _():
            for source in range(tall):

                @pl.when(source != level_at)
                def _():
                    arrive(from_lat.at[stream, source], stream * 6 + 2, source)

            total = own[stream]
            for source in range(tall):
                total = total + from_lat[stream, source].astype(F32)
            place = level_at - base
            chunk = block_of(0, True) * owners + place
            grad_ref[stream, core, chunk] = total.astype(grad_ref.dtype)
            mine = grad_ref.at[stream, core, chunk]
            for index in range(tall):
                to = far_level(index)

                @pl.when(to != level_at)
                def _():
                    send(mine, mine, stream * 6 + 3, index, place, (to * inner + row_at, lon))

            spread(stream, place)

    def start_spread(stream):
        for rank in range(owners):
            place = owner(rank) - base

            @pl.when(owner(rank) != level_at)
            def _():
                chunk = block_of(0, True) * owners + place
                arrive(grad_ref.at[stream, core, chunk], stream * 6 + 3, place)
                spread(stream, place)

    def start_pair_gather(stream):
        for rank in range(owners):
            place = owner(rank) - base
            for index in range(1, plane):
                mine = grad_ref.at[stream, core, block_of(index, False) * owners + place]
                arrive(mine, stream * 6 + 4, (index - 1) * owners + place)
                slot = index * owners + place
                send(mine, mine, stream * 6 + 5, slot, slot, pair)

    def finish(stream):
        spare = lat_out.at[stream, 0]
        for place in range(owners):
            for index in range(plane):
                chunk = block_of(index, False) * owners + place
                slot = index * owners + place
                arrive(grad_ref.at[stream, other, chunk], stream * 6 + 5, slot)
                drain(spare, stream * 6 + 5, slot)
                if index:
                    drain(spare, stream * 6 + 4, (index - 1) * owners + place)

            @pl.when(owner(place) != level_at)
            def _():
                drain(spare, stream * 6 + 2, place)

        @pl.when(owning)
        def _():
            for index in range(tall):

                @pl.when(far_level(index) != level_at)
                def _():
                    drain(spare, stream * 6 + 3, index)

    def pole_term(slot, start):
        return dot(wf[:, start : start + band], at_poles[slot], ((1,), (0,)))

    fill(0, accg, True)
    open_gap = jnp.zeros((hid, (rows - 1) * width), F32)
    for step in range(steps):
        extra = None
        if step == 0:
            extra = jnp.concatenate([pole_term(0, 2 * band), open_gap], axis=1)
        elif step == steps - 1:
            extra = jnp.concatenate([open_gap, pole_term(1, 0)], axis=1)
        second_step(step, extra)
        if step == 0:
            gen_copies = start_pair(0)
        if step == 2:
            gen_copies = start_lon(0, gen_copies)
    fill(1, accx, False)
    enc_copies = start_pair(1)

    for copy in hid_copies:
        copy.wait_send()
    for slot in range(2):
        arrive(hrow.at[slot * (height + 1)], 15, slot)

    def rebuild_step(step, packed):
        value = dot(wr[...], window(hrow, step * rows, 0, hid), ((1,), (0,)))
        for place in range(rows):
            row = step * rows + place
            lanes = slice(place * width, (place + 1) * width)
            left, centre, right = (value[tap * deep : (tap + 1) * deep, lanes] for tap in range(3))
            packed = packed + shifted(
                jnp.where(lane == width - 1, left, jnp.where(lane == 0, right, 0.0)), 2 * row + 1
            )
            inner = jnp.where(lane == 0, 0.0, shifted(left, 1))
            inner = inner + centre
            inner = inner + jnp.where(lane == width - 1, 0.0, shifted(right, -1))
            ysum[row] = inner
        return packed

    packed = jnp.zeros((deep, width), F32)
    enc_copies = start_lon(1, enc_copies)
    if levels > 1:
        met(levels - 1)
    start_lat(0, gen_copies)
    for step in range(steps):
        packed = rebuild_step(step, packed)
    ycol[...] = packed
    y_copies = [
        send(ycol, yhalo.at[0], 16, 0, 0, east),
        send(ycol, yhalo.at[1], 16, 1, 1, west),
    ]
    start_lat(1, enc_copies)

    def turn_out(load, target, size):
        for row in range(height):
            turned[row // 8, pl.ds(row % 8, size, stride=8), :] = load(row)
        kept = target.shape[0]
        target[...] = jnp.concatenate(
            [
                turned[part, : kept * 8].reshape(kept, 8, width)
                for part in range(height // 8)
            ],
            axis=1,
        ).astype(BF16)

    start_lat_gather(0)
    turn_out(lambda row: feat_rows[row].astype(F32), feat_ref, hid)
    for copy in y_copies:
        copy.wait()
    y_rims = jnp.where(lax.rem(lane, 2) == 0, shifted(yhalo[1], -1), shifted(yhalo[0], 1))

    def rebuilt_row(row):
        edges = shifted(y_rims, -(2 * row + 1))
        return ysum[row] + jnp.where((lane == 0) | (lane == width - 1), edges, 0.0)

    start_lat_gather(1)
    turn_out(rebuilt_row, reb_ref, deep)
    start_spread(0)
    start_spread(1)
    start_pair_gather(0)
    start_pair_gather(1)
    finish(0)
    finish(1)


def finish_kernel(norm, reb_in, feat_in, grad_in, reb_out, feat_out, enc_out, gen_out, flat, ready, sem):
    taps, count, hid = enc_out.shape
    side_lanes = hid // 2
    copies = [
        pltpu.make_async_copy(feat_in, feat_out, sem.at[0]),
        pltpu.make_async_copy(reb_in, reb_out, sem.at[1]),
    ]
    for copy in copies:
        copy.start()
    for stream, out in ((0, gen_out), (1, enc_out)):
        for side in range(2):
            gathered = grad_in[stream, side].astype(F32) * norm
            flat[:, side * side_lanes : (side + 1) * side_lanes] = gathered.reshape(-1, side_lanes)
        for tap in range(taps):
            ready[stream, tap] = flat[tap * count : (tap + 1) * count]
        copies.append(pltpu.make_async_copy(ready.at[stream], out, sem.at[2 + stream]))
        copies[-1].start()
    for copy in copies:
        copy.wait()


def on_device(fields, enc_kernel, gen_kernel, recon_grad):
    count, height, width = fields.shape
    hid = enc_kernel.shape[2]
    deep = -(-count // 16) * 16
    lats = lax.axis_size("lat")
    lons = lax.axis_size("lon")
    halves = lons // 2
    band = 3 * deep
    side_lanes = hid // 2
    inner = 2
    tall = lats // inner
    owners = tall // 2
    plane = halves * inner
    chunks = plane * owners
    per = -(-9 * count // (chunks * 8)) * 8
    hops = (plane - 1) * owners
    reach = inner * (tall - 1 - (tall - owners) // 2)
    levels = (reach - 1).bit_length()
    counts = [plane, hops, tall, tall, hops, chunks] * 2 + [2, 4, 4, 2, 2]
    vmem = pl.BlockSpec(memory_space=pltpu.VMEM)
    anywhere = pl.BlockSpec(memory_space=pltpu.HBM)
    rebuilt, feat, summed = pl.pallas_call(
        functools.partial(layer_kernel, lats, halves, deep),
        out_shape=[
            jax.ShapeDtypeStruct((count, height, width), BF16),
            jax.ShapeDtypeStruct((hid, height, width), BF16),
            jax.ShapeDtypeStruct((2, 2, chunks, per, side_lanes), BF16),
        ],
        in_specs=[anywhere] * 4,
        out_specs=[vmem] * 3,
        scratch_shapes=[
            pltpu.VMEM((2, count, height, width), BF16),
            pltpu.VMEM((2, 9, count, hid), BF16),
            pltpu.VMEM((2, height // 8, deep * 8, width), F32),
            pltpu.VMEM((height + 2, 2 * band, width), BF16),
            pltpu.VMEM((deep // 2, width), BF16),
            pltpu.VMEM((2, deep // 2, width), BF16),
            pltpu.VMEM((2, 2, deep // 2, width), BF16),
            pltpu.VMEM((height + 2, hid, width), BF16),
            pltpu.VMEM((height // 4, hid, 4 * width), F32),
            pltpu.VMEM((height, hid, width), BF16),
            pltpu.VMEM((2, 9, deep, hid), BF16),
            pltpu.VMEM((hid, 9 * deep), BF16),
            pltpu.VMEM((hid, 9 * deep), BF16),
            pltpu.VMEM((band, 3 * hid), BF16),
            pltpu.VMEM((height, deep, width), F32),
            pltpu.VMEM((deep, width), F32),
            pltpu.VMEM((2, deep, width), F32),
            pltpu.VMEM((height // 8, hid * 8, width), F32),
            pltpu.VMEM((9 * deep, hid), F32),
            pltpu.VMEM((9 * deep, hid), F32),
            pltpu.VMEM((2, 2, chunks * per, side_lanes), F32),
            pltpu.VMEM((2, chunks * per, side_lanes), F32),
            pltpu.VMEM((2, chunks, per, side_lanes), LINK),
            pltpu.VMEM((2, plane - 1, owners, per, side_lanes), LINK),
            pltpu.VMEM((2, owners, per, side_lanes), LINK),
            pltpu.VMEM((2, tall, per, side_lanes), LINK),
            pltpu.VMEM((2, per, side_lanes), F32),
            pltpu.SemaphoreType.DMA((4,)),
            pltpu.SemaphoreType.REGULAR((levels,)),
        ]
        + [pltpu.SemaphoreType.DMA((size,)) for size in counts for _ in range(2)],
        compiler_params=pltpu.CompilerParams(
            collective_id=0, has_side_effects=True, vmem_limit_bytes=48 << 20
        ),
    )(
        *(pltpu.with_memory_space_constraint(v, pltpu.HBM) for v in (
        fields,
        recon_grad,
        enc_kernel.transpose(0, 1, 3, 2).reshape(9, count, hid),
        gen_kernel.reshape(9, count, hid),
        ))
    )
    norm = 1.0 / float(height * lats * width * lons) ** 0.5
    rebuilt, feat, enc_grad, gen_grad = pl.pallas_call(
        functools.partial(finish_kernel, norm),
        out_shape=[
            jax.ShapeDtypeStruct((count, height, width), BF16),
            jax.ShapeDtypeStruct((hid, height, width), BF16),
            jax.ShapeDtypeStruct((9, count, hid), F32),
            jax.ShapeDtypeStruct((9, count, hid), F32),
        ],
        in_specs=[vmem] * 3,
        out_specs=[anywhere] * 4,
        scratch_shapes=[
            pltpu.VMEM((chunks * per, hid), F32),
            pltpu.VMEM((2, 9, count, hid), F32),
            pltpu.SemaphoreType.DMA((4,)),
        ],
        compiler_params=pltpu.CompilerParams(vmem_limit_bytes=8 << 20),
    )(rebuilt, feat, summed)
    return (
        rebuilt,
        feat,
        enc_grad.reshape(3, 3, count, hid).transpose(0, 1, 3, 2),
        gen_grad.reshape(3, 3, count, hid),
    )


def solution(mesh):
    return jax.shard_map(
        on_device,
        mesh=mesh,
        in_specs=(P(None, "lat", "lon"), P(), P(), P(None, "lat", "lon")),
        out_specs=(P(None, "lat", "lon"), P(None, "lat", "lon"), P(), P()),
        check_vma=False,
    )
```

```python
import functools

import jax
import jax.numpy as jnp
from jax import lax
from jax.experimental import pallas as pl
from jax.experimental.pallas import tpu as pltpu
from jax.sharding import PartitionSpec as P

MESH = pl.DeviceIdType.MESH
LINK = jnp.bfloat16
F32 = jnp.float32
BF16 = jnp.bfloat16


def dot(left, right, dims):
    return lax.dot_general(left, right, (dims, ((), ())), preferred_element_type=F32)


def shifted(value, amount):
    width = value.shape[1]
    if isinstance(amount, int):
        amount = amount % width
        if amount == 0:
            return value
    return pltpu.roll(value, amount, 1)


def layer_kernel(
    lats, halves, deep, f_hbm, g_hbm, we_hbm, wg_hbm, reb_ref, feat_ref, grad_ref,
    fin, win, flat, xg, colp, colh, corner, hrow, dact, feat_rows, wpad, we, wf, wr,
    ysum, ycol, yhalo, turned, pregrad, parts, from_pair, lon_out, from_lon, lat_out, from_lat, own,
    local_sem, greeted, *sems,
):
    count, height, width = fin.shape[1:]
    hid = hrow.shape[1]
    lons = 2 * halves
    band = 3 * deep
    half_deep = deep // 2
    lat = lax.axis_index("lat")
    lon = lax.axis_index("lon")
    half = lax.div(lon, 2)
    core = lax.rem(lon, 2)
    other = 1 - core
    below_top = lax.div(lat + lats - 1, lats)
    above_end = lax.div(2 * lats - 2 - lat, lats)

    inner = lats // from_lat.shape[1]
    plane = halves * inner
    level_at = lax.div(lat, inner)
    row_at = lax.rem(lat, inner)

    def plane_peer(index):
        turn, swap = divmod(index, inner)
        return (
            level_at * inner + lax.rem(row_at + swap, inner),
            lax.rem(half + turn, halves) * 2 + core,
        )

    def along(step):
        place = lat + step
        beyond = jnp.where((place < 0) | (place >= lats), 1, 0)
        mirrored = 2 * lats - 1 - place if step > 0 else -1 - place
        return (
            place + beyond * (mirrored - place),
            lax.rem(lon + beyond * halves, lons),
        )

    def greet(level):
        for step in (1 << level, -(1 << level)):
            pl.semaphore_signal(
                greeted.at[level], inc=1, device_id=along(step), device_id_type=MESH
            )

    def met(level):
        pl.semaphore_wait(greeted.at[level], 2)

    def north_of(place):
        return (lat - below_top, lax.rem(place + (1 - below_top) * halves, lons))

    def south_of(place):
        return (lat + above_end, lax.rem(place + (1 - above_end) * halves, lons))

    west_lon = lax.rem(lon + lons - 1, lons)
    east_lon = lax.rem(lon + 1, lons)
    pair = (lat, half * 2 + other)
    west = (lat, west_lon)
    east = (lat, east_lon)
    north = north_of(lon)
    south = south_of(lon)
    diagonals = [
        (south_of(east_lon), 1 - above_end, 0),
        (north_of(east_lon), below_top, 0),
        (south_of(west_lon), 1 - above_end, 1),
        (north_of(west_lon), below_top, 1),
    ]

    loads = [
        pltpu.make_async_copy(f_hbm, fin.at[0], local_sem.at[0]),
        pltpu.make_async_copy(g_hbm, fin.at[1], local_sem.at[1]),
        pltpu.make_async_copy(we_hbm, win.at[0], local_sem.at[2]),
        pltpu.make_async_copy(wg_hbm, win.at[1], local_sem.at[3]),
    ]
    for load in loads:
        load.start()

    barrier = pltpu.get_barrier_semaphore()
    peers = [west, east] + [peer for peer, slot, side in diagonals]
    peers += [plane_peer(index) for index in range(1, plane)]
    peers += [north, south]
    for peer in peers:
        pl.semaphore_signal(barrier, inc=1, device_id=peer, device_id_type=MESH)

    def send(src, dst, phase, send_slot, recv_slot, peer):
        copy = pltpu.make_async_remote_copy(
            src_ref=src,
            dst_ref=dst,
            send_sem=sems[2 * phase].at[send_slot],
            recv_sem=sems[2 * phase + 1].at[recv_slot],
            device_id=peer,
            device_id_type=MESH,
        )
        copy.start()
        return copy

    def arrive(ref, phase, slot):
        pltpu.make_async_copy(ref, ref, sems[2 * phase + 1].at[slot]).wait()

    def drain(ref, phase, slot):
        pltpu.make_async_copy(ref, ref, sems[2 * phase].at[slot]).wait()

    lane = lax.broadcasted_iota(jnp.int32, (deep, width), 1)
    half_lane = lax.broadcasted_iota(jnp.int32, (half_deep, width), 1)
    rim = (lane == 0) | (lane == width - 1)

    for array in range(2):
        for part in range(height // 8):
            flat[array, part, count * 8 :] = jnp.zeros(((deep - count) * 8, width), F32)
        wpad[array, :, deep - 16 :] = jnp.zeros((9, 16, hid), BF16)
    for load in loads[:2]:
        load.wait()
    for array in range(2):
        for part in range(height // 8):
            cells = fin[array, :, part * 8 : (part + 1) * 8].astype(F32)
            flat[array, part, : count * 8] = cells.reshape(count * 8, width)

    def cells_of(array, row):
        return flat[array, row // 8, pl.ds(row % 8, deep, stride=8), :]

    packed = jnp.zeros((half_deep, width), F32)
    for row in range(height):
        for array in range(2):
            cells = cells_of(array, row)
            xg[row + 1, array * band + deep : array * band + 2 * deep] = cells.astype(BF16)
            rims = jnp.where(rim, cells, 0.0)
            for part in range(2):
                packed = packed + shifted(
                    rims[part * half_deep : (part + 1) * half_deep],
                    2 * row + 1 + (2 * array + part) * 2 * height,
                )
    colp[...] = packed.astype(BF16)

    pl.semaphore_wait(barrier, len(peers))
    col_copies = [
        send(colp, colh.at[0], 12, 0, 0, east),
        send(colp, colh.at[1], 12, 1, 1, west),
    ]

    def send_rows(array):
        middle = pl.ds(array * band + deep, deep)
        return [
            send(
                xg.at[1, middle], xg.at[below_top * (height + 1), middle],
                13, 2 * array, 2 * array + below_top, north,
            ),
            send(
                xg.at[height, middle], xg.at[(1 - above_end) * (height + 1), middle],
                13, 2 * array + 1, 2 * array + 1 - above_end, south,
            ),
        ]

    row_copies = send_rows(0)
    corner_copies = [
        send(colp, corner.at[slot, side], 14, index, 2 * slot + side, peer)
        for index, (peer, slot, side) in enumerate(diagonals)
    ]
    row_copies += send_rows(1)
    levels = greeted.shape[0]
    greet(0)

    for load in loads[2:]:
        load.wait()
    for array in range(2):
        for tap in range(9):
            row_tap, col_tap = divmod(tap, 3)
            target = (2 - row_tap) * 3 + col_tap if array else tap
            wpad[array, target, :count] = win[array, tap]
    for tap in range(9):
        row_tap, col_tap = divmod(tap, 3)
        wr[col_tap * deep : (col_tap + 1) * deep, row_tap * hid : (row_tap + 1) * hid] = wpad[
            1, (2 - row_tap) * 3 + col_tap
        ]
    line = lax.broadcasted_iota(jnp.int32, (hid, hid), 0)
    column = lax.broadcasted_iota(jnp.int32, (hid, hid), 1)
    eye = jnp.where(line == column, 1.0, 0.0).astype(BF16)
    for array, target in ((0, we), (1, wf)):
        target[...] = dot(eye, wpad[array].reshape(9 * deep, hid), ((1,), (1,))).astype(BF16)

    even = lax.rem(half_lane, 2) == 0

    def join(from_west, from_east):
        return jnp.where(
            even, shifted(from_east.astype(F32), -1), shifted(from_west.astype(F32), 1)
        )

    def widen(array, slot, cells, rims, turn):
        parts_in = []
        for part in range(2):
            group = (2 * array + part) * 2 * height
            parts_in.append(shifted(rims, turn(group)))
        edges = jnp.concatenate(parts_in, axis=0)
        before = jnp.where(lane == 0, edges, shifted(cells, 1)).astype(BF16)
        after = jnp.where(lane == width - 1, edges, shifted(cells, -1)).astype(BF16)
        first, last = (after, before) if array else (before, after)
        base = array * band
        xg[slot, base : base + deep] = first
        xg[slot, base + 2 * deep : base + band] = last

    for copy in col_copies:
        copy.wait()
    own_rims = join(colh[0], colh[1])

    def centre_of(array, slot):
        return xg[slot, array * band + deep : array * band + 2 * deep].astype(F32)

    def widen_own(array):
        for row in range(height):
            widen(
                array, row + 1, centre_of(array, row + 1), own_rims,
                lambda group: -(2 * row + 1 + group),
            )

    source_rows = (below_top * (height - 1), (1 - above_end) * (height - 1))

    def widen_halo(array, halo_rims):
        middle = pl.ds(array * band + deep, deep)
        for slot in range(2):
            arrive(xg.at[slot * (height + 1), middle], 13, 2 * array + slot)
        for slot in range(2):
            cells = centre_of(array, slot * (height + 1))
            at = source_rows[slot]
            widen(
                array, slot * (height + 1), cells, halo_rims[slot],
                lambda group: lax.rem(2 * width - (2 * at + 1 + group), width),
            )

    rows = 4
    steps = height // rows

    def window(ref, row, start, size):
        return jnp.concatenate(
            [
                ref[pl.ds(row + place, 3), start : start + size].reshape(3 * size, width)
                for place in range(rows)
            ],
            axis=1,
        )

    def conv_step(step):
        row = step * rows
        pre_act = dot(we[...], window(xg, row, 0, band), ((1,), (0,)))
        logistic = 1.0 / (1.0 + jnp.exp(-pre_act))
        gated = pre_act * logistic
        dact[step] = logistic + gated * (1.0 - logistic)
        hidden = gated.astype(BF16)
        for place in range(rows):
            hrow[row + 1 + place] = hidden[:, place * width : (place + 1) * width]

    def second_step(step, extra):
        row = step * rows
        feat = dot(wf[...], window(xg, row, band, band), ((1,), (0,)))
        if extra is not None:
            feat = feat + extra
        feat = feat.astype(BF16)
        for place in range(rows):
            feat_rows[row + place] = feat[:, place * width : (place + 1) * width]
        pre_grad = (feat.astype(F32) * dact[step]).astype(BF16)
        pregrad[:, step * rows * width : (step + 1) * rows * width] = pre_grad

    widen_own(0)
    met(0)
    if levels > 1:
        greet(1)
    for step in range(1, steps - 1):
        conv_step(step)
    widen_own(1)
    for copy in corner_copies:
        copy.wait_send()
    for slot in range(4):
        arrive(corner.at[slot // 2, slot % 2], 14, slot)
    for copy in row_copies:
        copy.wait_send()
    halo_rims = [join(corner[slot, 0], corner[slot, 1]) for slot in range(2)]
    widen_halo(0, halo_rims)
    for level in range(1, levels - 1):
        met(level)
        greet(level + 1)
    conv_step(0)
    conv_step(steps - 1)
    hid_copies = [
        send(hrow.at[1], hrow.at[below_top * (height + 1)], 15, 0, below_top, north),
        send(hrow.at[height], hrow.at[(1 - above_end) * (height + 1)], 15, 1, 1 - above_end, south),
    ]
    widen_halo(1, halo_rims)
    ends = ((0, below_top, 2 * band, 0), (1, above_end, 0, height - 1))
    at_poles = []
    for slot, inside, start, row in ends:
        edge = xg[slot * (height + 1), band:]
        at_poles.append(jnp.where(inside == 0, edge, jnp.zeros_like(edge)))
        xg[slot * (height + 1), band:] = jnp.where(inside == 0, jnp.zeros_like(edge), edge)
    side_lanes = hid // 2
    per = lon_out.shape[2]
    owners = lat_out.shape[1]
    tall = from_lat.shape[1]
    base = (tall - owners) // 2
    upper = lax.div(2 * level_at, tall)
    owning = (level_at >= base) & (level_at < base + owners)
    for stream in range(2):
        from_lat[stream, level_at] = jnp.zeros(from_lat.shape[2:], LINK)

    def fill(stream, row_tap, value):
        for col_tap in range(3):
            tap = row_tap * 3 + col_tap
            for side in range(2):
                parts[stream, side, tap * count : (tap + 1) * count] = value[
                    col_tap * deep : col_tap * deep + count,
                    side * side_lanes : (side + 1) * side_lanes,
                ]

    def rows_at(place, start):
        return jnp.concatenate(
            [xg[row + place, start : start + band] for row in range(height)], axis=1
        )

    def piece(index, size):
        return pl.ds(pl.multiple_of(index * size, 8), size)

    def owner(index):
        return base + index + upper * (owners - 1 - 2 * index)

    def block_of(index, forward):
        turn, swap = divmod(index, inner)
        source = lax.rem(half + (turn if forward else halves - turn), halves)
        return source * inner + lax.rem(row_at + swap, inner)

    def start_pair(stream):
        copies = {}
        for index in list(range(plane - 1, 0, -1)) + [0]:
            part = piece(block_of(index, True), owners * per)
            copies[index] = send(
                parts.at[stream, other, part], from_pair.at[stream, part],
                stream * 6, index, index, pair,
            )
        return copies

    def start_lon(stream, copies):
        onward = {}
        for index in range(plane - 1, 0, -1):
            copies[index].wait()
            for rank in reversed(range(owners)):
                place = owner(rank) - base
                chunk = block_of(index, True) * owners + place
                part = piece(chunk, per)
                lon_out[stream, chunk] = (
                    parts[stream, core, part] + from_pair[stream, part]
                ).astype(LINK)
                slot = (index - 1) * owners + rank
                onward[index, rank] = send(
                    lon_out.at[stream, chunk],
                    from_lon.at[stream, index - 1, place],
                    stream * 6 + 1, slot, slot, plane_peer(index),
                )
        copies[0].wait()
        return onward

    def start_lat(stream, copies):
        for rank in reversed(range(owners)):
            to = owner(rank)
            place = to - base
            part = piece(block_of(0, True) * owners + place, per)
            total = parts[stream, core, part] + from_pair[stream, part]
            for index in range(plane - 1, 0, -1):
                copies[index, rank].wait()
                total = total + from_lon[stream, index - 1, place].astype(F32)
            lat_out[stream, place] = total.astype(LINK)

            @pl.when(to == level_at)
            def _():
                own[stream] = total

            @pl.when(to != level_at)
            def _():
                send(
                    lat_out.at[stream, place], from_lat.at[stream, level_at],
                    stream * 6 + 2, rank, level_at, (to * inner + row_at, lon),
                )

    def spread(stream, place):
        mine = grad_ref.at[stream, core, block_of(0, True) * owners + place]
        for index in range(plane - 1, 0, -1):
            slot = (index - 1) * owners + place
            send(mine, mine, stream * 6 + 4, slot, slot, plane_peer(index))
        send(mine, mine, stream * 6 + 5, place, place, pair)

    def far_level(index):
        rank = tall - 1 - index if index < tall // 2 else index - tall // 2
        return rank + upper * (tall - 1 - 2 * rank)

    def start_lat_gather(stream):
        @pl.when(owning)
        def _():
            for source in range(tall):

                @pl.when(source != level_at)
                def _():
                    arrive(from_lat.at[stream, source], stream * 6 + 2, source)

            total = own[stream]
            for source in range(tall):
                total = total + from_lat[stream, source].astype(F32)
            place = level_at - base
            chunk = block_of(0, True) * owners + place
            grad_ref[stream, core, chunk] = total.astype(grad_ref.dtype)
            mine = grad_ref.at[stream, core, chunk]
            for index in range(tall):
                to = far_level(index)

                @pl.when(to != level_at)
                def _():
                    send(mine, mine, stream * 6 + 3, index, place, (to * inner + row_at, lon))

            spread(stream, place)

    def start_spread(stream):
        for rank in range(owners):
            place = owner(rank) - base

            @pl.when(owner(rank) != level_at)
            def _():
                chunk = block_of(0, True) * owners + place
                arrive(grad_ref.at[stream, core, chunk], stream * 6 + 3, place)
                spread(stream, place)

    def start_pair_gather(stream):
        for rank in range(owners):
            place = owner(rank) - base
            for index in range(1, plane):
                mine = grad_ref.at[stream, core, block_of(index, False) * owners + place]
                arrive(mine, stream * 6 + 4, (index - 1) * owners + place)
                slot = index * owners + place
                send(mine, mine, stream * 6 + 5, slot, slot, pair)

    def finish(stream):
        spare = lat_out.at[stream, 0]
        for place in range(owners):
            for index in range(plane):
                chunk = block_of(index, False) * owners + place
                slot = index * owners + place
                arrive(grad_ref.at[stream, other, chunk], stream * 6 + 5, slot)
                drain(spare, stream * 6 + 5, slot)
                if index:
                    drain(spare, stream * 6 + 4, (index - 1) * owners + place)

            @pl.when(owner(place) != level_at)
            def _():
                drain(spare, stream * 6 + 2, place)

        @pl.when(owning)
        def _():
            for index in range(tall):

                @pl.when(far_level(index) != level_at)
                def _():
                    drain(spare, stream * 6 + 3, index)

    def pole_term(slot, start):
        return dot(wf[:, start : start + band], at_poles[slot], ((1,), (0,)))

    spare_rows = parts.shape[2] - 9 * count
    if spare_rows:
        for stream in range(2):
            for side in range(2):
                parts[stream, side, 9 * count :] = jnp.zeros((spare_rows, side_lanes), F32)
    hidden = jnp.concatenate([hrow[row + 1] for row in range(height)], axis=1)
    for place in range(3):
        value = dot(rows_at(place, band), hidden, ((1,), (1,)))
        for slot, inside, start, row in ends:
            if start == place * band:
                value = value + dot(at_poles[slot], hrow[row + 1], ((1,), (1,)))
        fill(0, 2 - place, value)
    open_gap = jnp.zeros((hid, (rows - 1) * width), F32)
    for step in range(steps):
        extra = None
        if step == 0:
            extra = jnp.concatenate([pole_term(0, 2 * band), open_gap], axis=1)
        elif step == steps - 1:
            extra = jnp.concatenate([open_gap, pole_term(1, 0)], axis=1)
        second_step(step, extra)
        if step == 0:
            gen_copies = start_pair(0)
        if step == 3:
            gen_copies = start_lon(0, gen_copies)
    for place in range(3):
        fill(1, place, dot(rows_at(place, 0), pregrad[...], ((1,), (1,))))
    enc_copies = start_pair(1)

    def rebuild_step(step, packed):
        value = dot(wr[...], window(hrow, step * rows, 0, hid), ((1,), (0,)))
        for place in range(rows):
            row = step * rows + place
            lanes = slice(place * width, (place + 1) * width)
            left, centre, right = (value[tap * deep : (tap + 1) * deep, lanes] for tap in range(3))
            packed = packed + shifted(
                jnp.where(lane == width - 1, left, jnp.where(lane == 0, right, 0.0)), 2 * row + 1
            )
            inner = jnp.where(lane == 0, 0.0, shifted(left, 1))
            inner = inner + centre
            inner = inner + jnp.where(lane == width - 1, 0.0, shifted(right, -1))
            ysum[row] = inner
        return packed

    packed = jnp.zeros((deep, width), F32)
    enc_copies = start_lon(1, enc_copies)
    if levels > 1:
        met(levels - 1)
    start_lat(0, gen_copies)
    for copy in hid_copies:
        copy.wait_send()
    for slot in range(2):
        arrive(hrow.at[slot * (height + 1)], 15, slot)
    for step in range(steps):
        packed = rebuild_step(step, packed)
    ycol[...] = packed
    y_copies = [
        send(ycol, yhalo.at[0], 16, 0, 0, east),
        send(ycol, yhalo.at[1], 16, 1, 1, west),
    ]
    start_lat(1, enc_copies)

    def turn_out(load, target, size):
        for row in range(height):
            turned[row // 8, pl.ds(row % 8, size, stride=8), :] = load(row)
        kept = target.shape[0]
        target[...] = jnp.concatenate(
            [
                turned[part, : kept * 8].reshape(kept, 8, width)
                for part in range(height // 8)
            ],
            axis=1,
        ).astype(BF16)

    start_lat_gather(0)
    turn_out(lambda row: feat_rows[row].astype(F32), feat_ref, hid)
    for copy in y_copies:
        copy.wait()
    y_rims = jnp.where(lax.rem(lane, 2) == 0, shifted(yhalo[1], -1), shifted(yhalo[0], 1))

    def rebuilt_row(row):
        edges = shifted(y_rims, -(2 * row + 1))
        return ysum[row] + jnp.where((lane == 0) | (lane == width - 1), edges, 0.0)

    start_lat_gather(1)
    turn_out(rebuilt_row, reb_ref, deep)
    start_spread(0)
    start_spread(1)
    start_pair_gather(0)
    start_pair_gather(1)
    finish(0)
    finish(1)


def finish_kernel(norm, reb_in, feat_in, grad_in, reb_out, feat_out, enc_out, gen_out, flat, ready, sem):
    taps, count, hid = enc_out.shape
    side_lanes = hid // 2
    copies = [
        pltpu.make_async_copy(feat_in, feat_out, sem.at[0]),
        pltpu.make_async_copy(reb_in, reb_out, sem.at[1]),
    ]
    for copy in copies:
        copy.start()
    for stream, out in ((0, gen_out), (1, enc_out)):
        for side in range(2):
            gathered = grad_in[stream, side].astype(F32) * norm
            flat[:, side * side_lanes : (side + 1) * side_lanes] = gathered.reshape(-1, side_lanes)
        for tap in range(taps):
            ready[stream, tap] = flat[tap * count : (tap + 1) * count]
        copies.append(pltpu.make_async_copy(ready.at[stream], out, sem.at[2 + stream]))
        copies[-1].start()
    for copy in copies:
        copy.wait()


def on_device(fields, enc_kernel, gen_kernel, recon_grad):
    count, height, width = fields.shape
    hid = enc_kernel.shape[2]
    deep = -(-count // 16) * 16
    lats = lax.axis_size("lat")
    lons = lax.axis_size("lon")
    halves = lons // 2
    band = 3 * deep
    side_lanes = hid // 2
    inner = 2
    tall = lats // inner
    owners = tall // 2
    plane = halves * inner
    chunks = plane * owners
    per = -(-9 * count // (chunks * 8)) * 8
    hops = (plane - 1) * owners
    reach = inner * (tall - 1 - (tall - owners) // 2)
    levels = (reach - 1).bit_length()
    counts = [plane, hops, tall, tall, hops, chunks] * 2 + [2, 4, 4, 2, 2]
    vmem = pl.BlockSpec(memory_space=pltpu.VMEM)
    anywhere = pl.BlockSpec(memory_space=pltpu.HBM)
    rebuilt, feat, summed = pl.pallas_call(
        functools.partial(layer_kernel, lats, halves, deep),
        out_shape=[
            jax.ShapeDtypeStruct((count, height, width), BF16),
            jax.ShapeDtypeStruct((hid, height, width), BF16),
            jax.ShapeDtypeStruct((2, 2, chunks, per, side_lanes), BF16),
        ],
        in_specs=[anywhere] * 4,
        out_specs=[vmem] * 3,
        scratch_shapes=[
            pltpu.VMEM((2, count, height, width), BF16),
            pltpu.VMEM((2, 9, count, hid), BF16),
            pltpu.VMEM((2, height // 8, deep * 8, width), F32),
            pltpu.VMEM((height + 2, 2 * band, width), BF16),
            pltpu.VMEM((deep // 2, width), BF16),
            pltpu.VMEM((2, deep // 2, width), BF16),
            pltpu.VMEM((2, 2, deep // 2, width), BF16),
            pltpu.VMEM((height + 2, hid, width), BF16),
            pltpu.VMEM((height // 4, hid, 4 * width), F32),
            pltpu.VMEM((height, hid, width), BF16),
            pltpu.VMEM((2, 9, deep, hid), BF16),
            pltpu.VMEM((hid, 9 * deep), BF16),
            pltpu.VMEM((hid, 9 * deep), BF16),
            pltpu.VMEM((band, 3 * hid), BF16),
            pltpu.VMEM((height, deep, width), F32),
            pltpu.VMEM((deep, width), F32),
            pltpu.VMEM((2, deep, width), F32),
            pltpu.VMEM((height // 8, hid * 8, width), F32),
            pltpu.VMEM((hid, height * width), BF16),
            pltpu.VMEM((2, 2, chunks * per, side_lanes), F32),
            pltpu.VMEM((2, chunks * per, side_lanes), F32),
            pltpu.VMEM((2, chunks, per, side_lanes), LINK),
            pltpu.VMEM((2, plane - 1, owners, per, side_lanes), LINK),
            pltpu.VMEM((2, owners, per, side_lanes), LINK),
            pltpu.VMEM((2, tall, per, side_lanes), LINK),
            pltpu.VMEM((2, per, side_lanes), F32),
            pltpu.SemaphoreType.DMA((4,)),
            pltpu.SemaphoreType.REGULAR((levels,)),
        ]
        + [pltpu.SemaphoreType.DMA((size,)) for size in counts for _ in range(2)],
        compiler_params=pltpu.CompilerParams(
            collective_id=0, has_side_effects=True, vmem_limit_bytes=48 << 20
        ),
    )(
        *(pltpu.with_memory_space_constraint(v, pltpu.HBM) for v in (
        fields,
        recon_grad,
        enc_kernel.transpose(0, 1, 3, 2).reshape(9, count, hid),
        gen_kernel.reshape(9, count, hid),
        ))
    )
    norm = 1.0 / float(height * lats * width * lons) ** 0.5
    rebuilt, feat, enc_grad, gen_grad = pl.pallas_call(
        functools.partial(finish_kernel, norm),
        out_shape=[
            jax.ShapeDtypeStruct((count, height, width), BF16),
            jax.ShapeDtypeStruct((hid, height, width), BF16),
            jax.ShapeDtypeStruct((9, count, hid), F32),
            jax.ShapeDtypeStruct((9, count, hid), F32),
        ],
        in_specs=[vmem] * 3,
        out_specs=[anywhere] * 4,
        scratch_shapes=[
            pltpu.VMEM((chunks * per, hid), F32),
            pltpu.VMEM((2, 9, count, hid), F32),
            pltpu.SemaphoreType.DMA((4,)),
        ],
        compiler_params=pltpu.CompilerParams(vmem_limit_bytes=8 << 20),
    )(rebuilt, feat, summed)
    return (
        rebuilt,
        feat,
        enc_grad.reshape(3, 3, count, hid).transpose(0, 1, 3, 2),
        gen_grad.reshape(3, 3, count, hid),
    )


def solution(mesh):
    return jax.shard_map(
        on_device,
        mesh=mesh,
        in_specs=(P(None, "lat", "lon"), P(), P(), P(None, "lat", "lon")),
        out_specs=(P(None, "lat", "lon"), P(None, "lat", "lon"), P(), P()),
        check_vma=False,
    )
```

```python
import functools

import jax
import jax.numpy as jnp
from jax import lax
from jax.experimental import pallas as pl
from jax.experimental.pallas import tpu as pltpu
from jax.sharding import PartitionSpec as P

MESH = pl.DeviceIdType.MESH
LINK = jnp.bfloat16
F32 = jnp.float32
BF16 = jnp.bfloat16


def dot(left, right, dims):
    return lax.dot_general(left, right, (dims, ((), ())), preferred_element_type=F32)


def shifted(value, amount):
    width = value.shape[1]
    if isinstance(amount, int):
        amount = amount % width
        if amount == 0:
            return value
    return pltpu.roll(value, amount, 1)


def layer_kernel(
    lats, halves, deep, f_hbm, g_hbm, we_hbm, wg_hbm, reb_ref, feat_ref, grad_ref,
    fin, win, flat, xg, colp, colh, corner, hrow, dact, feat_rows, wpad, we, wf, wr,
    ysum, ycol, yhalo, turned, pregrad, parts, from_pair, lon_out, from_lon, lat_out, from_lat, own,
    local_sem, greeted, *sems,
):
    count, height, width = fin.shape[1:]
    hid = hrow.shape[1]
    lons = 2 * halves
    band = 3 * deep
    half_deep = deep // 2
    lat = lax.axis_index("lat")
    lon = lax.axis_index("lon")
    half = lax.div(lon, 2)
    core = lax.rem(lon, 2)
    other = 1 - core
    below_top = lax.div(lat + lats - 1, lats)
    above_end = lax.div(2 * lats - 2 - lat, lats)

    inner = lats // from_lat.shape[1]
    plane = halves * inner
    level_at = lax.div(lat, inner)
    row_at = lax.rem(lat, inner)

    def plane_peer(index):
        turn, swap = divmod(index, inner)
        return (
            level_at * inner + lax.rem(row_at + swap, inner),
            lax.rem(half + turn, halves) * 2 + core,
        )

    def along(step):
        place = lat + step
        beyond = jnp.where((place < 0) | (place >= lats), 1, 0)
        mirrored = 2 * lats - 1 - place if step > 0 else -1 - place
        return (
            place + beyond * (mirrored - place),
            lax.rem(lon + beyond * halves, lons),
        )

    def greet(level):
        for step in (1 << level, -(1 << level)):
            pl.semaphore_signal(
                greeted.at[level], inc=1, device_id=along(step), device_id_type=MESH
            )

    def met(level):
        pl.semaphore_wait(greeted.at[level], 2)

    def north_of(place):
        return (lat - below_top, lax.rem(place + (1 - below_top) * halves, lons))

    def south_of(place):
        return (lat + above_end, lax.rem(place + (1 - above_end) * halves, lons))

    west_lon = lax.rem(lon + lons - 1, lons)
    east_lon = lax.rem(lon + 1, lons)
    pair = (lat, half * 2 + other)
    west = (lat, west_lon)
    east = (lat, east_lon)
    north = north_of(lon)
    south = south_of(lon)
    diagonals = [
        (south_of(east_lon), 1 - above_end, 0),
        (north_of(east_lon), below_top, 0),
        (south_of(west_lon), 1 - above_end, 1),
        (north_of(west_lon), below_top, 1),
    ]

    loads = [
        pltpu.make_async_copy(f_hbm, fin.at[0], local_sem.at[0]),
        pltpu.make_async_copy(g_hbm, fin.at[1], local_sem.at[1]),
        pltpu.make_async_copy(we_hbm, win.at[0], local_sem.at[2]),
        pltpu.make_async_copy(wg_hbm, win.at[1], local_sem.at[3]),
    ]
    for load in loads:
        load.start()

    barrier = pltpu.get_barrier_semaphore()
    peers = [west, east] + [peer for peer, slot, side in diagonals]
    peers += [plane_peer(index) for index in range(1, plane)]
    peers += [north, south]
    for peer in peers:
        pl.semaphore_signal(barrier, inc=1, device_id=peer, device_id_type=MESH)

    def send(src, dst, phase, send_slot, recv_slot, peer):
        copy = pltpu.make_async_remote_copy(
            src_ref=src,
            dst_ref=dst,
            send_sem=sems[2 * phase].at[send_slot],
            recv_sem=sems[2 * phase + 1].at[recv_slot],
            device_id=peer,
            device_id_type=MESH,
        )
        copy.start()
        return copy

    def arrive(ref, phase, slot):
        pltpu.make_async_copy(ref, ref, sems[2 * phase + 1].at[slot]).wait()

    def drain(ref, phase, slot):
        pltpu.make_async_copy(ref, ref, sems[2 * phase].at[slot]).wait()

    lane = lax.broadcasted_iota(jnp.int32, (deep, width), 1)
    half_lane = lax.broadcasted_iota(jnp.int32, (half_deep, width), 1)
    rim = (lane == 0) | (lane == width - 1)

    for array in range(2):
        for part in range(height // 8):
            flat[array, part, count * 8 :] = jnp.zeros(((deep - count) * 8, width), F32)
        wpad[array, :, deep - 16 :] = jnp.zeros((9, 16, hid), BF16)
    for load in loads[:2]:
        load.wait()
    for array in range(2):
        for part in range(height // 8):
            cells = fin[array, :, part * 8 : (part + 1) * 8].astype(F32)
            flat[array, part, : count * 8] = cells.reshape(count * 8, width)

    def cells_of(array, row):
        return flat[array, row // 8, pl.ds(row % 8, deep, stride=8), :]

    packed = jnp.zeros((half_deep, width), F32)
    for row in range(height):
        for array in range(2):
            cells = cells_of(array, row)
            xg[row + 1, array * band + deep : array * band + 2 * deep] = cells.astype(BF16)
            rims = jnp.where(rim, cells, 0.0)
            for part in range(2):
                packed = packed + shifted(
                    rims[part * half_deep : (part + 1) * half_deep],
                    2 * row + 1 + (2 * array + part) * 2 * height,
                )
    colp[...] = packed.astype(BF16)

    pl.semaphore_wait(barrier, len(peers))
    col_copies = [
        send(colp, colh.at[0], 12, 0, 0, east),
        send(colp, colh.at[1], 12, 1, 1, west),
    ]

    def send_rows(array):
        middle = pl.ds(array * band + deep, deep)
        return [
            send(
                xg.at[1, middle], xg.at[below_top * (height + 1), middle],
                13, 2 * array, 2 * array + below_top, north,
            ),
            send(
                xg.at[height, middle], xg.at[(1 - above_end) * (height + 1), middle],
                13, 2 * array + 1, 2 * array + 1 - above_end, south,
            ),
        ]

    row_copies = send_rows(0)
    corner_copies = [
        send(colp, corner.at[slot, side], 14, index, 2 * slot + side, peer)
        for index, (peer, slot, side) in enumerate(diagonals)
    ]
    row_copies += send_rows(1)
    levels = greeted.shape[0]
    greet(0)

    for load in loads[2:]:
        load.wait()
    for array in range(2):
        for tap in range(9):
            row_tap, col_tap = divmod(tap, 3)
            target = (2 - row_tap) * 3 + col_tap if array else tap
            wpad[array, target, :count] = win[array, tap]
    for tap in range(9):
        row_tap, col_tap = divmod(tap, 3)
        wr[col_tap * deep : (col_tap + 1) * deep, row_tap * hid : (row_tap + 1) * hid] = wpad[
            1, (2 - row_tap) * 3 + col_tap
        ]
    line = lax.broadcasted_iota(jnp.int32, (hid, hid), 0)
    column = lax.broadcasted_iota(jnp.int32, (hid, hid), 1)
    eye = jnp.where(line == column, 1.0, 0.0).astype(BF16)
    for array, target in ((0, we), (1, wf)):
        target[...] = dot(eye, wpad[array].reshape(9 * deep, hid), ((1,), (1,))).astype(BF16)

    even = lax.rem(half_lane, 2) == 0

    def join(from_west, from_east):
        return jnp.where(
            even, shifted(from_east.astype(F32), -1), shifted(from_west.astype(F32), 1)
        )

    def widen(array, slot, cells, rims, turn):
        parts_in = []
        for part in range(2):
            group = (2 * array + part) * 2 * height
            parts_in.append(shifted(rims, turn(group)))
        edges = jnp.concatenate(parts_in, axis=0)
        before = jnp.where(lane == 0, edges, shifted(cells, 1)).astype(BF16)
        after = jnp.where(lane == width - 1, edges, shifted(cells, -1)).astype(BF16)
        first, last = (after, before) if array else (before, after)
        base = array * band
        xg[slot, base : base + deep] = first
        xg[slot, base + 2 * deep : base + band] = last

    for copy in col_copies:
        copy.wait()
    own_rims = join(colh[0], colh[1])

    def centre_of(array, slot):
        return xg[slot, array * band + deep : array * band + 2 * deep].astype(F32)

    def widen_own(array):
        for row in range(height):
            widen(
                array, row + 1, centre_of(array, row + 1), own_rims,
                lambda group: -(2 * row + 1 + group),
            )

    source_rows = (below_top * (height - 1), (1 - above_end) * (height - 1))

    def widen_halo(array, halo_rims):
        middle = pl.ds(array * band + deep, deep)
        for slot in range(2):
            arrive(xg.at[slot * (height + 1), middle], 13, 2 * array + slot)
        for slot in range(2):
            cells = centre_of(array, slot * (height + 1))
            at = source_rows[slot]
            widen(
                array, slot * (height + 1), cells, halo_rims[slot],
                lambda group: lax.rem(2 * width - (2 * at + 1 + group), width),
            )

    rows = 4
    steps = height // rows

    def window(ref, row, start, size):
        return jnp.concatenate(
            [
                ref[pl.ds(row + place, 3), start : start + size].reshape(3 * size, width)
                for place in range(rows)
            ],
            axis=1,
        )

    def conv_step(step):
        row = step * rows
        pre_act = dot(we[...], window(xg, row, 0, band), ((1,), (0,)))
        logistic = 1.0 / (1.0 + jnp.exp(-pre_act))
        gated = pre_act * logistic
        dact[step] = logistic + gated * (1.0 - logistic)
        hidden = gated.astype(BF16)
        for place in range(rows):
            hrow[row + 1 + place] = hidden[:, place * width : (place + 1) * width]

    def second_step(step, extra):
        row = step * rows
        feat = dot(wf[...], window(xg, row, band, band), ((1,), (0,)))
        if extra is not None:
            feat = feat + extra
        feat = feat.astype(BF16)
        for place in range(rows):
            feat_rows[row + place] = feat[:, place * width : (place + 1) * width]
        pre_grad = (feat.astype(F32) * dact[step]).astype(BF16)
        pregrad[:, step * rows * width : (step + 1) * rows * width] = pre_grad

    widen_own(0)
    met(0)
    if levels > 1:
        greet(1)
    for step in range(1, steps - 1):
        conv_step(step)
    widen_own(1)
    for copy in corner_copies:
        copy.wait_send()
    for slot in range(4):
        arrive(corner.at[slot // 2, slot % 2], 14, slot)
    for copy in row_copies:
        copy.wait_send()
    halo_rims = [join(corner[slot, 0], corner[slot, 1]) for slot in range(2)]
    widen_halo(0, halo_rims)
    for level in range(1, levels - 1):
        met(level)
        greet(level + 1)
    conv_step(0)
    conv_step(steps - 1)
    hid_copies = [
        send(hrow.at[1], hrow.at[below_top * (height + 1)], 15, 0, below_top, north),
        send(hrow.at[height], hrow.at[(1 - above_end) * (height + 1)], 15, 1, 1 - above_end, south),
    ]
    widen_halo(1, halo_rims)
    ends = ((0, below_top, 2 * band, 0), (1, above_end, 0, height - 1))
    at_poles = []
    for slot, inside, start, row in ends:
        edge = xg[slot * (height + 1), band:]
        at_poles.append(jnp.where(inside == 0, edge, jnp.zeros_like(edge)))
        xg[slot * (height + 1), band:] = jnp.where(inside == 0, jnp.zeros_like(edge), edge)
    side_lanes = hid // 2
    per = lon_out.shape[2]
    owners = lat_out.shape[1]
    tall = from_lat.shape[1]
    base = (tall - owners) // 2
    upper = lax.div(2 * level_at, tall)
    owning = (level_at >= base) & (level_at < base + owners)
    for stream in range(2):
        from_lat[stream, level_at] = jnp.zeros(from_lat.shape[2:], LINK)

    def fill(stream, row_tap, value):
        for col_tap in range(3):
            tap = row_tap * 3 + col_tap
            for side in range(2):
                parts[stream, side, tap * count : (tap + 1) * count] = value[
                    col_tap * deep : col_tap * deep + count,
                    side * side_lanes : (side + 1) * side_lanes,
                ]

    def rows_at(place, start):
        return jnp.concatenate(
            [xg[row + place, start : start + band] for row in range(height)], axis=1
        )

    def piece(index, size):
        return pl.ds(pl.multiple_of(index * size, 8), size)

    def owner(index):
        return base + index + upper * (owners - 1 - 2 * index)

    def block_of(index, forward):
        turn, swap = divmod(index, inner)
        source = lax.rem(half + (turn if forward else halves - turn), halves)
        return source * inner + lax.rem(row_at + swap, inner)

    leaving = []

    def start_pair(stream):
        copies = {}
        for index in list(range(plane - 1, 0, -1)) + [0]:
            part = piece(block_of(index, True), owners * per)
            copies[index] = send(
                parts.at[stream, other, part], from_pair.at[stream, part],
                stream * 6, index, index, pair,
            )
        return copies

    def start_lon(stream, copies):
        onward = {}
        for index in range(plane - 1, 0, -1):
            copies[index].wait_recv()
            for rank in reversed(range(owners)):
                place = owner(rank) - base
                chunk = block_of(index, True) * owners + place
                part = piece(chunk, per)
                lon_out[stream, chunk] = (
                    parts[stream, core, part] + from_pair[stream, part]
                ).astype(LINK)
                slot = (index - 1) * owners + rank
                onward[index, rank] = send(
                    lon_out.at[stream, chunk],
                    from_lon.at[stream, index - 1, place],
                    stream * 6 + 1, slot, slot, plane_peer(index),
                )
        copies[0].wait_recv()
        leaving.extend(list(copies.values()) + list(onward.values()))
        return onward

    def start_lat(stream, copies):
        for rank in reversed(range(owners)):
            to = owner(rank)
            place = to - base
            part = piece(block_of(0, True) * owners + place, per)
            total = parts[stream, core, part] + from_pair[stream, part]
            for index in range(plane - 1, 0, -1):
                copies[index, rank].wait_recv()
                total = total + from_lon[stream, index - 1, place].astype(F32)
            lat_out[stream, place] = total.astype(LINK)

            @pl.when(to == level_at)
            def _():
                own[stream] = total

            @pl.when(to != level_at)
            def _():
                send(
                    lat_out.at[stream, place], from_lat.at[stream, level_at],
                    stream * 6 + 2, rank, level_at, (to * inner + row_at, lon),
                )

    def spread(stream, place):
        mine = grad_ref.at[stream, core, block_of(0, True) * owners + place]
        for index in range(plane - 1, 0, -1):
            slot = (index - 1) * owners + place
            send(mine, mine, stream * 6 + 4, slot, slot, plane_peer(index))
        send(mine, mine, stream * 6 + 5, place, place, pair)

    def far_level(index):
        rank = tall - 1 - index if index < tall // 2 else index - tall // 2
        return rank + upper * (tall - 1 - 2 * rank)

    def start_lat_gather(stream):
        @pl.when(owning)
        def _():
            for source in range(tall):

                @pl.when(source != level_at)
                def _():
                    arrive(from_lat.at[stream, source], stream * 6 + 2, source)

            total = own[stream]
            for source in range(tall):
                total = total + from_lat[stream, source].astype(F32)
            place = level_at - base
            chunk = block_of(0, True) * owners + place
            grad_ref[stream, core, chunk] = total.astype(grad_ref.dtype)
            mine = grad_ref.at[stream, core, chunk]
            for index in range(tall):
                to = far_level(index)

                @pl.when(to != level_at)
                def _():
                    send(mine, mine, stream * 6 + 3, index, place, (to * inner + row_at, lon))

            spread(stream, place)

    def start_spread(stream):
        for rank in range(owners):
            place = owner(rank) - base

            @pl.when(owner(rank) != level_at)
            def _():
                chunk = block_of(0, True) * owners + place
                arrive(grad_ref.at[stream, core, chunk], stream * 6 + 3, place)
                spread(stream, place)

    def start_pair_gather(stream):
        for rank in range(owners):
            place = owner(rank) - base
            for index in range(1, plane):
                mine = grad_ref.at[stream, core, block_of(index, False) * owners + place]
                arrive(mine, stream * 6 + 4, (index - 1) * owners + place)
                slot = index * owners + place
                send(mine, mine, stream * 6 + 5, slot, slot, pair)

    def finish(stream):
        spare = lat_out.at[stream, 0]
        for place in range(owners):
            for index in range(plane):
                chunk = block_of(index, False) * owners + place
                slot = index * owners + place
                arrive(grad_ref.at[stream, other, chunk], stream * 6 + 5, slot)
                drain(spare, stream * 6 + 5, slot)
                if index:
                    drain(spare, stream * 6 + 4, (index - 1) * owners + place)

            @pl.when(owner(place) != level_at)
            def _():
                drain(spare, stream * 6 + 2, place)

        @pl.when(owning)
        def _():
            for index in range(tall):

                @pl.when(far_level(index) != level_at)
                def _():
                    drain(spare, stream * 6 + 3, index)

    def pole_term(slot, start):
        return dot(wf[:, start : start + band], at_poles[slot], ((1,), (0,)))

    spare_rows = parts.shape[2] - 9 * count
    if spare_rows:
        for stream in range(2):
            for side in range(2):
                parts[stream, side, 9 * count :] = jnp.zeros((spare_rows, side_lanes), F32)
    hidden = jnp.concatenate([hrow[row + 1] for row in range(height)], axis=1)
    for place in range(3):
        value = dot(rows_at(place, band), hidden, ((1,), (1,)))
        for slot, inside, start, row in ends:
            if start == place * band:
                value = value + dot(at_poles[slot], hrow[row + 1], ((1,), (1,)))
        fill(0, 2 - place, value)
    open_gap = jnp.zeros((hid, (rows - 1) * width), F32)
    for step in range(steps):
        extra = None
        if step == 0:
            extra = jnp.concatenate([pole_term(0, 2 * band), open_gap], axis=1)
        elif step == steps - 1:
            extra = jnp.concatenate([open_gap, pole_term(1, 0)], axis=1)
        second_step(step, extra)
        if step == 0:
            gen_copies = start_pair(0)
        if step == 3:
            gen_copies = start_lon(0, gen_copies)
    for place in range(3):
        fill(1, place, dot(rows_at(place, 0), pregrad[...], ((1,), (1,))))
    enc_copies = start_pair(1)

    def rebuild_step(step, packed):
        value = dot(wr[...], window(hrow, step * rows, 0, hid), ((1,), (0,)))
        for place in range(rows):
            row = step * rows + place
            lanes = slice(place * width, (place + 1) * width)
            left, centre, right = (value[tap * deep : (tap + 1) * deep, lanes] for tap in range(3))
            packed = packed + shifted(
                jnp.where(lane == width - 1, left, jnp.where(lane == 0, right, 0.0)), 2 * row + 1
            )
            inner = jnp.where(lane == 0, 0.0, shifted(left, 1))
            inner = inner + centre
            inner = inner + jnp.where(lane == width - 1, 0.0, shifted(right, -1))
            ysum[row] = inner
        return packed

    packed = jnp.zeros((deep, width), F32)
    enc_copies = start_lon(1, enc_copies)
    if levels > 1:
        met(levels - 1)
    start_lat(0, gen_copies)
    for copy in hid_copies:
        copy.wait_send()
    for slot in range(2):
        arrive(hrow.at[slot * (height + 1)], 15, slot)
    for step in range(steps):
        packed = rebuild_step(step, packed)
    ycol[...] = packed
    y_copies = [
        send(ycol, yhalo.at[0], 16, 0, 0, east),
        send(ycol, yhalo.at[1], 16, 1, 1, west),
    ]
    start_lat(1, enc_copies)

    def turn_out(load, target, size):
        for row in range(height):
            turned[row // 8, pl.ds(row % 8, size, stride=8), :] = load(row)
        kept = target.shape[0]
        target[...] = jnp.concatenate(
            [
                turned[part, : kept * 8].reshape(kept, 8, width)
                for part in range(height // 8)
            ],
            axis=1,
        ).astype(BF16)

    start_lat_gather(0)
    turn_out(lambda row: feat_rows[row].astype(F32), feat_ref, hid)
    for copy in y_copies:
        copy.wait()
    y_rims = jnp.where(lax.rem(lane, 2) == 0, shifted(yhalo[1], -1), shifted(yhalo[0], 1))

    def rebuilt_row(row):
        edges = shifted(y_rims, -(2 * row + 1))
        return ysum[row] + jnp.where((lane == 0) | (lane == width - 1), edges, 0.0)

    start_lat_gather(1)
    turn_out(rebuilt_row, reb_ref, deep)
    start_spread(0)
    start_spread(1)
    start_pair_gather(0)
    start_pair_gather(1)
    finish(0)
    finish(1)
    for copy in leaving:
        copy.wait_send()


def finish_kernel(norm, reb_in, feat_in, grad_in, reb_out, feat_out, enc_out, gen_out, flat, ready, sem):
    taps, count, hid = enc_out.shape
    side_lanes = hid // 2
    copies = [
        pltpu.make_async_copy(feat_in, feat_out, sem.at[0]),
        pltpu.make_async_copy(reb_in, reb_out, sem.at[1]),
    ]
    for copy in copies:
        copy.start()
    for stream, out in ((0, gen_out), (1, enc_out)):
        for side in range(2):
            gathered = grad_in[stream, side].astype(F32) * norm
            flat[:, side * side_lanes : (side + 1) * side_lanes] = gathered.reshape(-1, side_lanes)
        for tap in range(taps):
            ready[stream, tap] = flat[tap * count : (tap + 1) * count]
        copies.append(pltpu.make_async_copy(ready.at[stream], out, sem.at[2 + stream]))
        copies[-1].start()
    for copy in copies:
        copy.wait()


def on_device(fields, enc_kernel, gen_kernel, recon_grad):
    count, height, width = fields.shape
    hid = enc_kernel.shape[2]
    deep = -(-count // 16) * 16
    lats = lax.axis_size("lat")
    lons = lax.axis_size("lon")
    halves = lons // 2
    band = 3 * deep
    side_lanes = hid // 2
    inner = 2
    tall = lats // inner
    owners = tall // 2
    plane = halves * inner
    chunks = plane * owners
    per = -(-9 * count // (chunks * 8)) * 8
    hops = (plane - 1) * owners
    reach = inner * (tall - 1 - (tall - owners) // 2)
    levels = (reach - 1).bit_length()
    counts = [plane, hops, tall, tall, hops, chunks] * 2 + [2, 4, 4, 2, 2]
    vmem = pl.BlockSpec(memory_space=pltpu.VMEM)
    anywhere = pl.BlockSpec(memory_space=pltpu.HBM)
    rebuilt, feat, summed = pl.pallas_call(
        functools.partial(layer_kernel, lats, halves, deep),
        out_shape=[
            jax.ShapeDtypeStruct((count, height, width), BF16),
            jax.ShapeDtypeStruct((hid, height, width), BF16),
            jax.ShapeDtypeStruct((2, 2, chunks, per, side_lanes), BF16),
        ],
        in_specs=[anywhere] * 4,
        out_specs=[vmem] * 3,
        scratch_shapes=[
            pltpu.VMEM((2, count, height, width), BF16),
            pltpu.VMEM((2, 9, count, hid), BF16),
            pltpu.VMEM((2, height // 8, deep * 8, width), F32),
            pltpu.VMEM((height + 2, 2 * band, width), BF16),
            pltpu.VMEM((deep // 2, width), BF16),
            pltpu.VMEM((2, deep // 2, width), BF16),
            pltpu.VMEM((2, 2, deep // 2, width), BF16),
            pltpu.VMEM((height + 2, hid, width), BF16),
            pltpu.VMEM((height // 4, hid, 4 * width), F32),
            pltpu.VMEM((height, hid, width), BF16),
            pltpu.VMEM((2, 9, deep, hid), BF16),
            pltpu.VMEM((hid, 9 * deep), BF16),
            pltpu.VMEM((hid, 9 * deep), BF16),
            pltpu.VMEM((band, 3 * hid), BF16),
            pltpu.VMEM((height, deep, width), F32),
            pltpu.VMEM((deep, width), F32),
            pltpu.VMEM((2, deep, width), F32),
            pltpu.VMEM((height // 8, hid * 8, width), F32),
            pltpu.VMEM((hid, height * width), BF16),
            pltpu.VMEM((2, 2, chunks * per, side_lanes), F32),
            pltpu.VMEM((2, chunks * per, side_lanes), F32),
            pltpu.VMEM((2, chunks, per, side_lanes), LINK),
            pltpu.VMEM((2, plane - 1, owners, per, side_lanes), LINK),
            pltpu.VMEM((2, owners, per, side_lanes), LINK),
            pltpu.VMEM((2, tall, per, side_lanes), LINK),
            pltpu.VMEM((2, per, side_lanes), F32),
            pltpu.SemaphoreType.DMA((4,)),
            pltpu.SemaphoreType.REGULAR((levels,)),
        ]
        + [pltpu.SemaphoreType.DMA((size,)) for size in counts for _ in range(2)],
        compiler_params=pltpu.CompilerParams(
            collective_id=0, has_side_effects=True, vmem_limit_bytes=48 << 20
        ),
    )(
        *(pltpu.with_memory_space_constraint(v, pltpu.HBM) for v in (
        fields,
        recon_grad,
        enc_kernel.transpose(0, 1, 3, 2).reshape(9, count, hid),
        gen_kernel.reshape(9, count, hid),
        ))
    )
    norm = 1.0 / float(height * lats * width * lons) ** 0.5
    rebuilt, feat, enc_grad, gen_grad = pl.pallas_call(
        functools.partial(finish_kernel, norm),
        out_shape=[
            jax.ShapeDtypeStruct((count, height, width), BF16),
            jax.ShapeDtypeStruct((hid, height, width), BF16),
            jax.ShapeDtypeStruct((9, count, hid), F32),
            jax.ShapeDtypeStruct((9, count, hid), F32),
        ],
        in_specs=[vmem] * 3,
        out_specs=[anywhere] * 4,
        scratch_shapes=[
            pltpu.VMEM((chunks * per, hid), F32),
            pltpu.VMEM((2, 9, count, hid), F32),
            pltpu.SemaphoreType.DMA((4,)),
        ],
        compiler_params=pltpu.CompilerParams(vmem_limit_bytes=8 << 20),
    )(rebuilt, feat, summed)
    return (
        rebuilt,
        feat,
        enc_grad.reshape(3, 3, count, hid).transpose(0, 1, 3, 2),
        gen_grad.reshape(3, 3, count, hid),
    )


def solution(mesh):
    return jax.shard_map(
        on_device,
        mesh=mesh,
        in_specs=(P(None, "lat", "lon"), P(), P(), P(None, "lat", "lon")),
        out_specs=(P(None, "lat", "lon"), P(None, "lat", "lon"), P(), P()),
        check_vma=False,
    )
```
